512 devices in a mesh: seq: 64 (over y, z_lo, core), head: 8 (over x, z_hi).
Axes of the slice: x: 4, y: 8, z: 8 (z_hi: 2, z_lo: 4; z = z_hi * 4 + z_lo), core: 2. Of those that a mesh axis runs over, the one named last changes fastest.
Arguments:
- mixer_query: bfloat16 [16384, 4096], P('seq', 'head'), may hold values from -13 to 13
- mixer_key: bfloat16 [16384, 4096], P('seq', 'head'), may hold values from -6 to 6
- mixer_value: bfloat16 [16384, 4096], P('seq', 'head'), may hold values from -6 to 6
- shift_taps: float32 [8, 4096], P(None, 'head'), may hold values from -2 to 2
- conv_kernel: float32 [4096, 16384], P(('head', 'seq')), may hold values from -2 to 2
- heads_query: bfloat16 [16384, 4096], P('seq', 'head'), may hold values from -6 to 6
- heads_key: bfloat16 [16384, 4096], P('seq', 'head'), may hold values from -6 to 6
- heads_value: bfloat16 [16384, 4096], P('seq', 'head'), may hold values from -6 to 6
- beta_attention: float32 [4096], P('head'), may hold values from 0.5 to 2
- beta_mixer: float32 [4096], P('head'), may hold values from 0.5 to 2
Outputs:
- block_output: bfloat16 [16384, 4096], P('seq', 'head')
The draws below stay inside these ranges and needn't reach their ends.
All inputs are finite; a program needn't handle non-finite values.
Results may differ from the reference program's by a relative error of at most 0.0053.
Values may be sent and summed in bfloat16 or wider, within the bound.
No kernel may reach another device: no remote copies, remote signals or barrier semaphores. Data moves between devices by JAX's collectives and lax.ppermute only.
A program may use at most 64 MiB of HBM per device.

```python
import math
import jax
import jax.numpy as jnp
from jax import lax

D = 4096
HD = 128
TAPS = 8
SPAN = 3
TOK_DEV = 256
LENGTH = 16384


def clipped(key, shape, bound):
    return jnp.clip(jax.random.normal(key, shape, jnp.float32), -bound, bound)


def attention_pair(key):
    base_query = clipped(jax.random.fold_in(key, 11), (LENGTH, D), 4.0)
    base_key = clipped(jax.random.fold_in(key, 12), (LENGTH, D), 4.0)
    return (base_query, base_key)


def draw_heads_query(key, part):
    return attention_pair(key)[0].astype(jnp.bfloat16)


def draw_heads_key(key, part):
    return attention_pair(key)[1].astype(jnp.bfloat16)


def draw_mixer_query(key, part):
    values = clipped(key, (LENGTH, D), 4.0)
    column = jnp.arange(D, dtype=jnp.float32)[None, :] / D
    return (values * 0.5 * jnp.exp(column * math.log(3.0))).astype(jnp.bfloat16)


def draw_conv_kernel(key, part):
    pick = jax.random.uniform(jax.random.fold_in(key, 1), (D, 1), jnp.float32)
    slow = jnp.exp(jax.random.uniform(jax.random.fold_in(key, 2), (D, 1), jnp.float32, math.log(0.25 / LENGTH), math.log(2.0 / LENGTH)))
    fast = jnp.exp(jax.random.uniform(jax.random.fold_in(key, 3), (D, 1), jnp.float32, math.log(1.0 / 50.0), math.log(1.0 / 25.0)))
    noise = clipped(jax.random.fold_in(key, 4), (D, LENGTH), 6.0)
    places = jnp.arange(LENGTH, dtype=jnp.float32)[None, :]
    rate = jnp.where(pick < 0.5, slow, fast)
    envelope = jnp.sqrt(2.0 * rate) * jnp.exp(-rate * places)
    return envelope * noise


def shard_levels(own_key, extent, cuts, low, top_value):
    level, own = 1.0, jax.random.fold_in(own_key, 6)
    for position, shards_of in cuts:
        heights = jnp.exp(jax.random.uniform(jax.random.fold_in(own, position), (shards_of,), jnp.float32, low / len(cuts), top_value / len(cuts)))
        level = level * jnp.repeat(heights, extent[position] // shards_of).reshape([-1 if axis == position else 1 for axis in range(len(extent))])
    return level


def gaussian(key, dims, spread, limit, pieces=(), held_as=jnp.bfloat16):
    entries = spread * jax.random.normal(key, dims, jnp.float32)
    if pieces:
        entries = entries * shard_levels(key, dims, pieces, -0.22, 0.18)
    return jnp.clip(entries, -limit, limit).astype(held_as)


def setup_inputs(seed: int = 0) -> dict:
    key_list = jax.random.split(jax.random.key(seed), 11)
    mixer_query = draw_mixer_query(jax.random.fold_in(key_list[10], 71), 0)
    mixer_key = gaussian(key_list[1], (LENGTH, D), 1.0, 6.0, ((0, 64), (1, 8)))
    mixer_value = gaussian(key_list[2], (LENGTH, D), 1.0, 6.0, ((0, 64), (1, 8)))
    shift_taps = gaussian(key_list[3], (TAPS, D), TAPS ** -0.5, 2.0, ((1, 8),), jnp.float32)
    conv_kernel = draw_conv_kernel(jax.random.fold_in(key_list[10], 71), 0)
    heads_query = draw_heads_query(jax.random.fold_in(key_list[10], 71), 0)
    heads_key = draw_heads_key(jax.random.fold_in(key_list[10], 71), 0)
    heads_value = gaussian(key_list[7], (LENGTH, D), 1.0, 6.0, ((0, 64), (1, 8)))
    beta_attention = jnp.clip(jnp.exp(math.log(2.0) - 1.3862944 * jax.random.uniform(key_list[8], (D,), jnp.float32) ** shard_levels(key_list[8], (D,), ((0, 8),), -0.2, 0.2)), 0.5, 2.0)
    beta_mixer = jnp.clip(jnp.exp(math.log(2.0) - 1.3862944 * jax.random.uniform(key_list[9], (D,), jnp.float32) ** shard_levels(key_list[9], (D,), ((0, 8),), -0.2, 0.2)), 0.5, 2.0)
    return dict(mixer_query=mixer_query, mixer_key=mixer_key, mixer_value=mixer_value, shift_taps=shift_taps, conv_kernel=conv_kernel, heads_query=heads_query, heads_key=heads_key, heads_value=heads_value, beta_attention=beta_attention, beta_mixer=beta_mixer)


def shift_conv(keys, taps):
    count = keys.shape[0]
    width = taps.shape[0]
    source = jnp.concatenate([jnp.zeros((width - 1, keys.shape[1]), jnp.float32), keys.astype(jnp.float32)], 0)
    total = jnp.zeros((count, keys.shape[1]), jnp.float32)
    for offset in range(width):
        total = total + taps[offset][None, :] * source[width - 1 - offset:width - 1 - offset + count]
    return total

def long_conv(signal, kernel):
    length = signal.shape[1]
    period = 2 * length
    group = 64
    number = signal.shape[0] // group

    def one(pair):
        part_signal, part_kernel = pair
        spectrum = jnp.fft.rfft(part_signal, n=period, axis=1) * jnp.fft.rfft(part_kernel, n=period, axis=1)
        return jnp.fft.irfft(spectrum, n=period, axis=1)[:, :length]
    result = lax.map(one, (signal.reshape(number, group, length), kernel.reshape(number, group, length)))
    return result.reshape(signal.shape[0], length)

def attention(query, keys, values):
    length, width = query.shape
    heads = width // HD
    scale = 1.0 / math.sqrt(HD)
    front = SPAN * TOK_DEV
    pad_keys = jnp.concatenate([jnp.zeros((front, width), keys.dtype), keys], 0)
    pad_values = jnp.concatenate([jnp.zeros((front, width), values.dtype), values], 0)

    def block(index):
        start = (index * TOK_DEV).astype(jnp.int32)
        rows_query = lax.dynamic_slice_in_dim(query, start, TOK_DEV, 0).astype(jnp.float32).reshape(TOK_DEV, heads, HD)
        rows_key = lax.dynamic_slice_in_dim(pad_keys, start, front + TOK_DEV, 0).astype(jnp.float32).reshape(front + TOK_DEV, heads, HD)
        rows_value = lax.dynamic_slice_in_dim(pad_values, start, front + TOK_DEV, 0).astype(jnp.float32).reshape(front + TOK_DEV, heads, HD)
        scores = jnp.einsum('qhd,khd->hqk', rows_query, rows_key, precision=lax.Precision.HIGHEST) * scale
        query_pos = start + jnp.arange(TOK_DEV, dtype=jnp.int32)
        key_pos = start - front + jnp.arange(front + TOK_DEV, dtype=jnp.int32)
        visible = (key_pos[None, :] <= query_pos[:, None]) & (key_pos[None, :] >= 0)
        scores = jnp.where(visible[None], scores, -1e+30)
        top = lax.optimization_barrier(jnp.max(scores, axis=2, keepdims=True))
        probs = jnp.exp(scores - top)
        weights = lax.optimization_barrier(probs.astype(jnp.bfloat16)).astype(jnp.float32)
        numer = jnp.einsum('hqk,khd->qhd', weights, rows_value, precision=lax.Precision.HIGHEST)
        total = lax.optimization_barrier(jnp.sum(probs, axis=2))
        return (numer / jnp.transpose(total)[:, :, None]).reshape(TOK_DEV, width)
    blocks = jnp.arange(length // TOK_DEV, dtype=jnp.int32)
    return lax.map(block, blocks).reshape(length, width)

def reference(mixer_query, mixer_key, mixer_value, shift_taps, conv_kernel, heads_query, heads_key, heads_value, beta_attention, beta_mixer):
    shifted = shift_conv(mixer_key, shift_taps)
    ssm_input = (shifted * mixer_value.astype(jnp.float32)).astype(jnp.bfloat16)
    signal = jnp.transpose(ssm_input).astype(jnp.float32)
    ssm_output = jnp.transpose(long_conv(signal, conv_kernel)).astype(jnp.bfloat16)
    mixer_branch = mixer_query.astype(jnp.float32) * ssm_output.astype(jnp.float32)
    attention_branch = attention(heads_query, heads_key, heads_value)
    attention_square = lax.optimization_barrier(jnp.sum(attention_branch * attention_branch, axis=1, keepdims=True)) / D
    mixer_square = lax.optimization_barrier(jnp.sum(mixer_branch * mixer_branch, axis=1, keepdims=True)) / D
    joined = beta_attention[None, :] * attention_branch * lax.rsqrt(attention_square + 1e-05) + beta_mixer[None, :] * mixer_branch * lax.rsqrt(mixer_square + 1e-05)
    return (joined * 0.5).astype(jnp.bfloat16)
```

```python
import math

import jax
import jax.numpy as jnp
import numpy as np
from jax import lax
from jax.experimental import pallas as pl
from jax.experimental.pallas import tpu as pltpu
from jax.sharding import PartitionSpec as P


D = 4096
HD = 128
TAPS = 8
SPAN = 3
RADIX = 128
F32 = jnp.float32
BF16 = jnp.bfloat16


def split_table(table):
    high = table.astype(np.float32).astype(jnp.bfloat16)
    low = (table - high.astype(np.float64)).astype(np.float32).astype(jnp.bfloat16)
    return high, low


def conv_tables(tokens):
    half = tokens // RADIX
    place = np.arange(RADIX)
    order = (place % (RADIX // half)) * half + place // (RADIX // half)
    freq = np.arange(RADIX) + 0.5
    one = 2.0 * np.pi * np.outer(freq, order) / (2 * RADIX)
    first = np.concatenate([np.cos(one), -np.sin(one)], 0)
    last = np.concatenate([np.cos(one), -np.sin(one)], 0).T * (1.0 / (RADIX * RADIX))
    first_natural = 2.0 * np.pi * np.outer(freq, place) / (2 * RADIX)
    first_natural = np.concatenate([np.cos(first_natural), -np.sin(first_natural)], 0)
    twist = 2.0 * np.pi * np.outer(freq, place) / (2 * RADIX * RADIX)
    two = 2.0 * np.pi * np.outer(place, place) / RADIX
    cos, sin = np.cos(two), np.sin(two)
    ahead = np.block([[cos, -sin], [sin, cos]])
    back = np.block([[cos, sin], [-sin, cos]])
    return dict(
        first=split_table(first),
        first_natural=split_table(first_natural),
        last=split_table(last),
        ahead=split_table(ahead),
        back=split_table(back),
        twist_cos=np.cos(twist).astype(np.float32),
        twist_sin=np.sin(twist).astype(np.float32),
    )


def halves(value):
    high = value.astype(BF16)
    return high, (value - high.astype(F32)).astype(BF16)


def mm(left, right):
    return lax.dot_general(left, right, (((1,), (0,)), ((), ())), preferred_element_type=F32)


def kernel_call(body, out_shape, scratch=(), vmem=None):
    def call(*args):
        return pl.pallas_call(
            body,
            out_shape=out_shape,
            scratch_shapes=list(scratch),
            compiler_params=pltpu.CompilerParams(vmem_limit_bytes=vmem or 48 * 2**20),
        )(*args)

    return call


def shift_body(before_ref, key_ref, value_ref, taps_ref, out_ref, ext_ref):
    count, _ = key_ref.shape
    ext_ref[0:8, :] = before_ref[...].astype(F32)
    ext_ref[8:, :] = key_ref[...].astype(F32)
    taps = taps_ref[...]
    total = taps[0:1, :] * ext_ref[8 : 8 + count, :]
    for j in range(1, TAPS):
        total = total + taps[j : j + 1, :] * ext_ref[8 - j : 8 - j + count, :]
    product = total * value_ref[...].astype(F32)
    out_ref[...] = product.T.astype(BF16).reshape(out_ref.shape)


def spectrum(first_step, twist_cos, twist_sin, ahead_hi, ahead_lo):
    real, imag = first_step[:RADIX], first_step[RADIX:]
    turned = jnp.concatenate(
        [real * twist_cos + imag * twist_sin, imag * twist_cos - real * twist_sin], 1
    )
    high, low = halves(turned)
    return mm(high, ahead_hi) + mm(low, ahead_hi) + mm(high, ahead_lo)


def kernel_spectrum_body(kernel_ref, fh_ref, fl_ref, tc_ref, ts_ref, ah_ref, al_ref, out_ref, rows_ref):
    channels = kernel_ref.shape[0]
    for a in range(RADIX):
        rows_ref[a * channels : (a + 1) * channels, :] = kernel_ref[:, a * RADIX : (a + 1) * RADIX]
    for c in range(channels):
        data = rows_ref[pl.ds(c, RADIX, stride=channels), :]
        high, low = halves(data)
        step = mm(fh_ref[...], high) + mm(fh_ref[...], low) + mm(fl_ref[...], high)
        out_ref[c] = spectrum(step, tc_ref[...], ts_ref[...], ah_ref[...], al_ref[...])


def filter_body(
    signal_ref, spec_ref, fh_ref, fl_ref, lh_ref, ll_ref, tc_ref, ts_ref, ah_ref, al_ref, bh_ref, bl_ref, out_ref, rows_ref, back_ref
):
    sources, channels, tokens = signal_ref.shape
    half = tokens // RADIX
    rows = sources * channels
    data = signal_ref[...].astype(F32).reshape(rows, tokens)
    for h in range(half):
        rows_ref[h * rows : (h + 1) * rows, :] = data[:, h * RADIX : (h + 1) * RADIX]
    tc, ts = tc_ref[...], ts_ref[...]
    for c in range(channels):
        data = rows_ref[pl.ds(c, RADIX, stride=channels), :].astype(BF16)
        step = mm(fh_ref[...], data) + mm(fl_ref[...], data)
        both = spectrum(step, tc, ts, ah_ref[...], al_ref[...])
        sig_r, sig_i = both[:, :RADIX], both[:, RADIX:]
        spec = spec_ref[c]
        ker_r, ker_i = spec[:, :RADIX], spec[:, RADIX:]
        high, low = halves(
            jnp.concatenate([sig_r * ker_r - sig_i * ker_i, sig_r * ker_i + sig_i * ker_r], 1)
        )
        back = mm(high, bh_ref[...]) + mm(low, bh_ref[...]) + mm(high, bl_ref[...])
        real, imag = back[:, :RADIX], back[:, RADIX:]
        high, low = halves(jnp.concatenate([real * tc - imag * ts, imag * tc + real * ts], 0))
        result = mm(lh_ref[...], high) + mm(lh_ref[...], low) + mm(ll_ref[...], high)
        back_ref[pl.ds(c, RADIX, stride=channels), :] = result
    joined = jnp.concatenate([back_ref[h * rows : (h + 1) * rows, :] for h in range(half)], 1)
    out_ref[...] = joined.astype(BF16).reshape(out_ref.shape)


def attention_body(block_ref, query_ref, key_ref, value_ref, one_ref, two_ref, three_ref, out_ref, sum_ref):
    count, width = query_ref.shape
    block = block_ref[0]
    earlier = (three_ref, two_ref, one_ref)
    row = lax.broadcasted_iota(jnp.int32, (count, count), 0)
    col = lax.broadcasted_iota(jnp.int32, (count, count), 1)
    causal = col <= row
    squares = jnp.zeros((count, HD), F32)
    for h in range(width // HD):
        lanes = slice(h * HD, (h + 1) * HD)
        query = query_ref[:, lanes]
        keys = jnp.concatenate([ref[0:count, lanes] for ref in earlier] + [key_ref[:, lanes]], 0)
        values = jnp.concatenate([ref[count:, lanes] for ref in earlier] + [value_ref[:, lanes]], 0)
        scores = lax.dot_general(query, keys, (((1,), (1,)), ((), ())), preferred_element_type=F32) * (
            1.0 / math.sqrt(HD)
        )
        parts = []
        for i in range(SPAN):
            seen = scores[:, i * count : (i + 1) * count]
            parts.append(jnp.where(block >= SPAN - i, seen, -1e30))
        parts.append(jnp.where(causal, scores[:, SPAN * count :], -1e30))
        scores = jnp.concatenate(parts, 1)
        top = jnp.max(scores, axis=1, keepdims=True)
        probs = jnp.exp(scores - top)
        total = jnp.sum(probs, axis=1, keepdims=True)
        numer = mm(probs.astype(BF16), values)
        branch = numer / total
        out_ref[:, lanes] = branch
        squares = squares + branch * branch
    sum_ref[...] = squares.T


def attend(block, query, key, value, one, two, three):
    count, width = query.shape
    vmem = pl.BlockSpec(memory_space=pltpu.VMEM)
    return pl.pallas_call(
        attention_body,
        out_shape=(jax.ShapeDtypeStruct((count, width), F32), jax.ShapeDtypeStruct((HD, count), F32)),
        in_specs=[pl.BlockSpec(memory_space=pltpu.SMEM)] + [vmem] * 6,
        out_specs=(vmem, vmem),
        compiler_params=pltpu.CompilerParams(vmem_limit_bytes=48 * 2**20),
        name="attention",
    )(block, query, key, value, one, two, three)


def sums_body(returned_ref, query_t_ref, att_ref, out_ref):
    mixed = returned_ref[...].astype(F32).reshape(query_t_ref.shape) * query_t_ref[...].astype(F32)
    mixer = jnp.sum(mixed * mixed, axis=0, keepdims=True)
    attention = jnp.sum(att_ref[...], axis=0, keepdims=True)
    rows = jnp.concatenate(
        [attention[:, :RADIX], attention[:, RADIX:], mixer[:, :RADIX], mixer[:, RADIX:], jnp.zeros((4, RADIX), F32)], 0
    )
    out_ref[...] = jnp.broadcast_to(rows[None], out_ref.shape)


def mixed_body(returned_ref, query_ref, beta_ref, out_ref):
    count, width = query_ref.shape
    returned = returned_ref[...].astype(F32).reshape(width, count).T
    out_ref[...] = query_ref[...].astype(F32) * returned * beta_ref[...]


def join_body(sums_ref, att_ref, mixed_ref, beta_ref, out_ref):
    count, _ = att_ref.shape
    total = sums_ref[0]
    for peer in range(1, sums_ref.shape[0]):
        total = total + sums_ref[peer]
    scale = lax.rsqrt(total * (1.0 / D) + 1e-05) * 0.5
    columns = jnp.concatenate([scale, jnp.zeros((RADIX - 8, RADIX), F32)], 0).T
    for h in range(count // RADIX):
        rows = slice(h * RADIX, (h + 1) * RADIX)
        attention_scale = columns[:, h : h + 1]
        mixer_scale = columns[:, 2 + h : 3 + h]
        out_ref[rows, :] = (
            beta_ref[...] * att_ref[rows, :] * attention_scale + mixed_ref[rows, :] * mixer_scale
        ).astype(BF16)


def transpose_body(in_ref, out_ref):
    out_ref[...] = in_ref[...].astype(F32).T.astype(BF16)


def mixer(
    mixer_query,
    mixer_key,
    mixer_value,
    shift_taps,
    conv_kernel,
    heads_query,
    heads_key,
    heads_value,
    beta_attention,
    beta_mixer,
):
    count, width = mixer_key.shape
    blocks = lax.axis_size("seq")
    peers = lax.axis_size("head")
    channels = width // blocks
    sds = jax.ShapeDtypeStruct
    tables = conv_tables(count)
    tables = {k: tuple(jnp.asarray(x) for x in v) if isinstance(v, tuple) else jnp.asarray(v) for k, v in tables.items()}
    onward = [(i, i + 1) for i in range(blocks - 1)]

    before = lax.ppermute(mixer_key[count - 8 :], "seq", onward)
    signal = kernel_call(
        shift_body, sds((blocks, channels, count), BF16), [pltpu.VMEM((count + 8, width), F32)]
    )(before, mixer_key, mixer_value, shift_taps)
    received = lax.all_to_all(signal, "seq", 0, 0, tiled=True)
    kernel_spectrum = kernel_call(
        kernel_spectrum_body, sds((channels, RADIX, 2 * RADIX), F32), [pltpu.VMEM((channels * RADIX, RADIX), F32)]
    )(conv_kernel, *tables["first_natural"], tables["twist_cos"], tables["twist_sin"], *tables["ahead"])
    filtered = kernel_call(
        filter_body, sds((blocks, channels, count), BF16), [pltpu.VMEM((channels * RADIX, RADIX), F32)] * 2
    )(
        received,
        kernel_spectrum,
        *tables["first"],
        *tables["last"],
        tables["twist_cos"],
        tables["twist_sin"],
        *tables["ahead"],
        *tables["back"],
    )
    returned = lax.all_to_all(filtered, "seq", 0, 0, tiled=True)

    carried = jnp.concatenate([heads_key, heads_value], 0)
    earlier = []
    for _ in range(SPAN):
        carried = lax.ppermute(carried, "seq", onward)
        earlier.append(carried)
    block = lax.axis_index("seq").astype(jnp.int32).reshape(1)
    attention_branch, attention_squares = attend(block, heads_query, heads_key, heads_value, *earlier)
    query_t = kernel_call(transpose_body, sds((width, count), BF16))(mixer_query)
    sums = kernel_call(sums_body, sds((peers, 8, RADIX), F32))(returned, query_t, attention_squares)
    gathered = lax.all_to_all(sums, "head", 0, 0, tiled=True)
    mixed = kernel_call(mixed_body, sds((count, width), F32))(
        returned, mixer_query, beta_mixer[None, :]
    )
    return kernel_call(join_body, sds((count, width), BF16))(gathered, attention_branch, mixed, beta_attention[None, :])


def solution(mesh):
    return jax.shard_map(
        mixer,
        mesh=mesh,
        in_specs=(
            P("seq", "head"),
            P("seq", "head"),
            P("seq", "head"),
            P(None, "head"),
            P(("head", "seq"), None),
            P("seq", "head"),
            P("seq", "head"),
            P("seq", "head"),
            P("head"),
            P("head"),
        ),
        out_specs=P("seq", "head"),
        check_vma=False,
    )
```

```python
import functools
import math

import jax
import jax.numpy as jnp
import numpy as np
from jax import lax
from jax.experimental import pallas as pl
from jax.experimental.pallas import tpu as pltpu
from jax.sharding import PartitionSpec as P


D = 4096
HD = 128
TAPS = 8
SPAN = 3
RADIX = 128
F32 = jnp.float32
BF16 = jnp.bfloat16


def split_table(table):
    high = table.astype(np.float32).astype(jnp.bfloat16)
    low = (table - high.astype(np.float64)).astype(np.float32).astype(jnp.bfloat16)
    return high, low


def conv_tables(tokens):
    half = tokens // RADIX
    place = np.arange(RADIX)
    order = (place % (RADIX // half)) * half + place // (RADIX // half)
    freq = np.arange(RADIX) + 0.5
    one = 2.0 * np.pi * np.outer(freq, order) / (2 * RADIX)
    first = np.concatenate([np.cos(one), -np.sin(one)], 0)
    last = first.T * (1.0 / (RADIX * RADIX))
    twist = 2.0 * np.pi * np.outer(freq, place) / (2 * RADIX * RADIX)
    two = 2.0 * np.pi * np.outer(place, place) / RADIX
    cos, sin = np.cos(two), np.sin(two)
    ahead = np.block([[cos, -sin], [sin, cos]])
    back = np.block([[cos, sin], [-sin, cos]])
    products = [
        np.concatenate(split_table(first), 1),
        np.concatenate(split_table(last), 0),
        *split_table(ahead),
        *split_table(back),
    ]
    return jnp.asarray(np.stack(products)), jnp.asarray(
        np.stack([np.cos(twist), np.sin(twist)]).astype(np.float32)
    )


def halves(value):
    high = value.astype(BF16)
    return high, (value - high.astype(F32)).astype(BF16)


def mm(left, right):
    return lax.dot_general(left, right, (((1,), (0,)), ((), ())), preferred_element_type=F32)


def kernel_call(body, out_shape, scratch=(), vmem=None):
    def call(*args):
        return pl.pallas_call(
            body,
            out_shape=out_shape,
            scratch_shapes=list(scratch),
            compiler_params=pltpu.CompilerParams(vmem_limit_bytes=vmem or 48 * 2**20),
        )(*args)

    return call


def shift_body(key_ref, value_ref, taps_ref, out_ref, ext_ref):
    count, width = key_ref.shape
    ext_ref[0:8, :] = jnp.zeros((8, width), F32)
    ext_ref[8 : 8 + count, :] = key_ref[...].astype(F32)
    taps = taps_ref[...]
    total = taps[0:1, :] * ext_ref[8 : 8 + count, :]
    for j in range(1, TAPS):
        total = total + taps[j : j + 1, :] * ext_ref[8 - j : 8 - j + count, :]
    product = total * value_ref[...].astype(F32)
    edges = jnp.concatenate(
        [
            ext_ref[8:16, :],
            ext_ref[count : 8 + count, :],
            value_ref[0:16, :].astype(F32)[0:8],
            jnp.zeros((RADIX - 24, width), F32),
        ],
        0,
    )
    shape = out_ref.shape[:2]
    out_ref[:, :, 0:count] = product.T.astype(BF16).reshape(*shape, count)
    out_ref[:, :, count:] = edges.T.astype(BF16).reshape(*shape, RADIX)


def product3(value, table_hi, table_lo):
    high, low = halves(value)
    return mm(high, table_hi) + mm(low, table_hi) + mm(high, table_lo)


def spectrum(step, tables_ref, twist_ref):
    cos, sin = twist_ref[0], twist_ref[1]
    turned = []
    for c in range(step.shape[1] // RADIX):
        lanes = slice(c * RADIX, (c + 1) * RADIX)
        real, imag = step[:RADIX, lanes], step[RADIX:, lanes]
        turned.append(jnp.concatenate([real * cos + imag * sin, imag * cos - real * sin], 1))
    return product3(jnp.concatenate(turned, 0), tables_ref[2], tables_ref[3])


def gather_rows(rows_ref, channels):
    return jnp.concatenate([rows_ref[pl.ds(c, RADIX, stride=channels), :] for c in range(channels)], 1)


def kernel_spectrum_body(half, kernel_ref, tables_ref, twist_ref, out_ref, rows_ref):
    channels = kernel_ref.shape[0]
    for a in range(RADIX):
        row = ((a % half) * (RADIX // half) + a // half) * channels
        rows_ref[row : row + channels, :] = kernel_ref[:, a * RADIX : (a + 1) * RADIX]
    high, low = halves(gather_rows(rows_ref, channels))
    first_hi, first_lo = tables_ref[0, :, :RADIX], tables_ref[0, :, RADIX:]
    step = mm(first_hi, high) + mm(first_hi, low) + mm(first_lo, high)
    out_ref[...] = spectrum(step, tables_ref, twist_ref)


def first_tokens(signal_ref, taps_ref, count):
    own = signal_ref[:, :, count:].astype(F32)
    head = signal_ref[:, :, :RADIX].astype(F32)
    previous = jnp.concatenate([jnp.zeros_like(own[:1]), own[:-1]], 0)
    sources, channels = own.shape[:2]
    own, previous, head = (x.reshape(sources * channels, RADIX) for x in (own, previous, head))
    lane = lax.broadcasted_iota(jnp.int32, own.shape, 1)
    window = jnp.where(lane < 16, previous, pltpu.roll(own, 16, 1))
    total = jnp.zeros_like(window)
    for j in range(TAPS):
        tap = jnp.broadcast_to(taps_ref[j][None], (sources, channels, RADIX)).reshape(window.shape)
        total = total + tap * (pltpu.roll(window, j, 1) if j else window)
    return jnp.where(lane < 8, pltpu.roll(total * own, RADIX - 16, 1), head)


def filter_body(signal_ref, taps_ref, spec_ref, tables_ref, twist_ref, out_ref, rows_ref, back_ref):
    sources, channels, count = out_ref.shape
    half = count // RADIX
    rows = sources * channels
    rows_ref[:rows, :] = first_tokens(signal_ref, taps_ref, count)
    for h in range(1, half):
        part = signal_ref[:, :, h * RADIX : (h + 1) * RADIX].astype(F32)
        rows_ref[h * rows : (h + 1) * rows, :] = part.reshape(rows, RADIX)
    data = gather_rows(rows_ref, channels).astype(BF16)
    step = mm(tables_ref[0], jnp.concatenate([data, data], 0))
    both = spectrum(step, tables_ref, twist_ref)
    sig_r, sig_i = both[:, :RADIX], both[:, RADIX:]
    ker_r, ker_i = spec_ref[:, :RADIX], spec_ref[:, RADIX:]
    both = jnp.concatenate([sig_r * ker_r - sig_i * ker_i, sig_r * ker_i + sig_i * ker_r], 1)
    both = product3(both, tables_ref[4], tables_ref[5])
    cos, sin = twist_ref[0], twist_ref[1]
    turned = []
    for c in range(channels):
        lines = slice(c * RADIX, (c + 1) * RADIX)
        real, imag = both[lines, :RADIX], both[lines, RADIX:]
        turned.append(jnp.concatenate([real * cos - imag * sin, imag * cos + real * sin], 0))
    high, low = halves(jnp.concatenate(turned, 1))
    last_hi, last_lo = tables_ref[1, :RADIX], tables_ref[1, RADIX:]
    result = mm(last_hi, high) + mm(last_hi, low) + mm(last_lo, high)
    for c in range(channels):
        back_ref[pl.ds(c, RADIX, stride=channels), :] = result[:, c * RADIX : (c + 1) * RADIX]
    for h in range(half):
        part = back_ref[h * rows : (h + 1) * rows, :].astype(BF16)
        out_ref[:, :, h * RADIX : (h + 1) * RADIX] = part.reshape(sources, channels, RADIX)


def attention_body(block_ref, query_ref, key_ref, value_ref, one_ref, two_ref, three_ref, out_ref, sum_ref):
    count, width = query_ref.shape
    block = block_ref[0]
    earlier = (three_ref, two_ref, one_ref)
    row = lax.broadcasted_iota(jnp.int32, (count, count), 0)
    col = lax.broadcasted_iota(jnp.int32, (count, count), 1)
    causal = col <= row
    squares = jnp.zeros((count, HD), F32)
    for h in range(width // HD):
        lanes = slice(h * HD, (h + 1) * HD)
        query = query_ref[:, lanes]
        keys = jnp.concatenate([ref[0:count, lanes] for ref in earlier] + [key_ref[:, lanes]], 0)
        values = jnp.concatenate([ref[count:, lanes] for ref in earlier] + [value_ref[:, lanes]], 0)
        scores = lax.dot_general(query, keys, (((1,), (1,)), ((), ())), preferred_element_type=F32) * (
            1.0 / math.sqrt(HD)
        )
        parts = []
        for i in range(SPAN):
            seen = scores[:, i * count : (i + 1) * count]
            parts.append(jnp.where(block >= SPAN - i, seen, -1e30))
        parts.append(jnp.where(causal, scores[:, SPAN * count :], -1e30))
        scores = jnp.concatenate(parts, 1)
        top = jnp.max(scores, axis=1, keepdims=True)
        probs = jnp.exp(scores - top)
        total = jnp.sum(probs, axis=1, keepdims=True)
        numer = mm(probs.astype(BF16), values)
        branch = numer / total
        out_ref[:, lanes] = branch
        squares = squares + branch * branch
    sum_ref[...] = squares.T


def attend(block, query, key, value, one, two, three):
    count, width = query.shape
    vmem = pl.BlockSpec(memory_space=pltpu.VMEM)
    return pl.pallas_call(
        attention_body,
        out_shape=(jax.ShapeDtypeStruct((count, width), F32), jax.ShapeDtypeStruct((HD, count), F32)),
        in_specs=[pl.BlockSpec(memory_space=pltpu.SMEM)] + [vmem] * 6,
        out_specs=(vmem, vmem),
        compiler_params=pltpu.CompilerParams(vmem_limit_bytes=48 * 2**20),
        name="attention",
    )(block, query, key, value, one, two, three)


def sums_body(returned_ref, query_t_ref, att_ref, out_ref):
    mixed = returned_ref[...].astype(F32).reshape(query_t_ref.shape) * query_t_ref[...].astype(F32)
    mixer = jnp.sum(mixed * mixed, axis=0, keepdims=True)
    attention = jnp.sum(att_ref[...], axis=0, keepdims=True)
    rows = jnp.concatenate(
        [attention[:, :RADIX], attention[:, RADIX:], mixer[:, :RADIX], mixer[:, RADIX:], jnp.zeros((4, RADIX), F32)], 0
    )
    out_ref[...] = jnp.broadcast_to(rows[None], out_ref.shape)


def mixed_body(returned_ref, query_ref, beta_ref, out_ref):
    count, width = query_ref.shape
    returned = returned_ref[...].astype(F32).reshape(width, count).T
    out_ref[...] = query_ref[...].astype(F32) * returned * beta_ref[...]


def join_body(sums_ref, att_ref, mixed_ref, beta_ref, out_ref):
    count, _ = att_ref.shape
    total = sums_ref[0]
    for peer in range(1, sums_ref.shape[0]):
        total = total + sums_ref[peer]
    scale = lax.rsqrt(total * (1.0 / D) + 1e-05) * 0.5
    columns = jnp.concatenate([scale, jnp.zeros((RADIX - 8, RADIX), F32)], 0).T
    for h in range(count // RADIX):
        rows = slice(h * RADIX, (h + 1) * RADIX)
        attention_scale = columns[:, h : h + 1]
        mixer_scale = columns[:, 2 + h : 3 + h]
        out_ref[rows, :] = (
            beta_ref[...] * att_ref[rows, :] * attention_scale + mixed_ref[rows, :] * mixer_scale
        ).astype(BF16)


def transpose_body(in_ref, out_ref):
    out_ref[...] = in_ref[...].astype(F32).T.astype(BF16)


def mixer(
    mixer_query,
    mixer_key,
    mixer_value,
    shift_taps,
    conv_kernel,
    heads_query,
    heads_key,
    heads_value,
    beta_attention,
    beta_mixer,
):
    count, width = mixer_key.shape
    blocks = lax.axis_size("seq")
    peers = lax.axis_size("head")
    channels = width // blocks
    sds = jax.ShapeDtypeStruct
    tables, twist = conv_tables(count)
    onward = [(i, i + 1) for i in range(blocks - 1)]
    seq = lax.axis_index("seq")

    signal = kernel_call(
        shift_body, sds((blocks, channels, count + RADIX), BF16), [pltpu.VMEM((count + 8, width), F32)]
    )(mixer_key, mixer_value, shift_taps)
    received = lax.all_to_all(signal, "seq", 0, 0, tiled=True)
    own_taps = lax.dynamic_slice(shift_taps, (0, seq * channels), (TAPS, channels))
    own_taps = jnp.broadcast_to(own_taps[:, :, None], (TAPS, channels, RADIX))
    rows = pltpu.VMEM((channels * RADIX, RADIX), F32)
    kernel_spectrum = kernel_call(
        functools.partial(kernel_spectrum_body, count // RADIX), sds((channels * RADIX, 2 * RADIX), F32), [rows]
    )(conv_kernel, tables, twist)
    filtered = kernel_call(
        filter_body, sds((blocks, channels, count), BF16), [rows, rows]
    )(received, own_taps, kernel_spectrum, tables, twist)
    returned = lax.all_to_all(filtered, "seq", 0, 0, tiled=True)

    carried = jnp.concatenate([heads_key, heads_value], 0)
    earlier = []
    for _ in range(SPAN):
        carried = lax.ppermute(carried, "seq", onward)
        earlier.append(carried)
    block = seq.astype(jnp.int32).reshape(1)
    attention_branch, attention_squares = attend(block, heads_query, heads_key, heads_value, *earlier)
    query_t = kernel_call(transpose_body, sds((width, count), BF16))(mixer_query)
    sums = kernel_call(sums_body, sds((peers, 8, RADIX), F32))(returned, query_t, attention_squares)
    gathered = lax.all_to_all(sums, "head", 0, 0, tiled=True)
    mixed = kernel_call(mixed_body, sds((count, width), F32))(
        returned, mixer_query, beta_mixer[None, :]
    )
    return kernel_call(join_body, sds((count, width), BF16))(gathered, attention_branch, mixed, beta_attention[None, :])


def solution(mesh):
    return jax.shard_map(
        mixer,
        mesh=mesh,
        in_specs=(
            P("seq", "head"),
            P("seq", "head"),
            P("seq", "head"),
            P(None, "head"),
            P(("head", "seq"), None),
            P("seq", "head"),
            P("seq", "head"),
            P("seq", "head"),
            P("head"),
            P("head"),
        ),
        out_specs=P("seq", "head"),
        check_vma=False,
    )
```

```python
import functools
import math

import jax
import jax.numpy as jnp
import numpy as np
from jax import lax
from jax.experimental import pallas as pl
from jax.experimental.pallas import tpu as pltpu
from jax.sharding import PartitionSpec as P


D = 4096
HD = 128
TAPS = 8
SPAN = 3
SIDE = 4
RADIX = 128
VMEM_LIMIT = 20 * 2**20
F32 = jnp.float32
BF16 = jnp.bfloat16


def split_table(table):
    high = table.astype(np.float32).astype(jnp.bfloat16)
    low = (table - high.astype(np.float64)).astype(np.float32).astype(jnp.bfloat16)
    return high, low


def conv_tables(tokens):
    half = tokens // RADIX
    place = np.arange(RADIX)
    order = (place % (RADIX // half)) * half + place // (RADIX // half)
    freq = np.arange(RADIX) + 0.5
    one = 2.0 * np.pi * np.outer(freq, order) / (2 * RADIX)
    first = np.concatenate([np.cos(one), -np.sin(one)], 0)
    last = first.T * (1.0 / (RADIX * RADIX))
    twist = 2.0 * np.pi * np.outer(freq, place) / (2 * RADIX * RADIX)
    two = 2.0 * np.pi * np.outer(place, place) / RADIX
    cos, sin = np.cos(two), np.sin(two)
    ahead = np.block([[cos, -sin], [sin, cos]])
    back = np.block([[cos, sin], [-sin, cos]])
    products = [
        np.concatenate(split_table(first), 1),
        np.concatenate(split_table(last), 0),
        *split_table(ahead),
        *split_table(back),
        np.concatenate(split_table(np.concatenate([np.cos(twist), np.sin(twist)], 1)), 0),
    ]
    return jnp.asarray(np.stack(products))


def halves(value):
    high = value.astype(BF16)
    return high, (value - high.astype(F32)).astype(BF16)


def mm(left, right):
    return lax.dot_general(left, right, (((1,), (0,)), ((), ())), preferred_element_type=F32)


def kernel_call(body, out_shape, scratch=()):
    def call(*args):
        return pl.pallas_call(
            body,
            out_shape=out_shape,
            scratch_shapes=list(scratch),
            compiler_params=pltpu.CompilerParams(vmem_limit_bytes=VMEM_LIMIT),
        )(*args)

    return call


def shift_body(key_ref, value_ref, taps_ref, out_ref, ext_ref):
    count, width = key_ref.shape
    ext_ref[0:8, :] = jnp.zeros((8, width), F32)
    ext_ref[8 : 8 + count, :] = key_ref[...].astype(F32)
    taps = taps_ref[...]
    total = taps[0:1, :] * ext_ref[8 : 8 + count, :]
    for j in range(1, TAPS):
        total = total + taps[j : j + 1, :] * ext_ref[8 - j : 8 - j + count, :]
    product = total * value_ref[...].astype(F32)
    edges = jnp.concatenate(
        [
            ext_ref[8:16, :],
            ext_ref[count : 8 + count, :],
            value_ref[0:16, :].astype(F32)[0:8],
            jnp.zeros((RADIX - 24, width), F32),
        ],
        0,
    )
    blocks, lines = out_ref.shape[:2]
    product = product.T.reshape(blocks, SIDE, lines, count)
    edges = edges.T.reshape(blocks, SIDE, lines, RADIX)
    for i in range(SIDE):
        out_ref[:, :, i * count : (i + 1) * count] = product[:, i].astype(BF16)
    joined = jnp.concatenate([edges[:, i, :, : RADIX // SIDE] for i in range(SIDE)], 2)
    out_ref[:, :, SIDE * count :] = joined.astype(BF16)


def product3(value, table_hi, table_lo):
    high, low = halves(value)
    return mm(high, table_hi) + mm(low, table_hi) + mm(high, table_lo)


def twists(tables_ref):
    table = tables_ref[6].astype(F32)
    table = table[:RADIX] + table[RADIX:]
    return table[:, :RADIX], table[:, RADIX:]


def spectrum(step, tables_ref):
    cos, sin = twists(tables_ref)
    turned = []
    for c in range(step.shape[1] // RADIX):
        lanes = slice(c * RADIX, (c + 1) * RADIX)
        real, imag = step[:RADIX, lanes], step[RADIX:, lanes]
        turned.append(jnp.concatenate([real * cos + imag * sin, imag * cos - real * sin], 1))
    return product3(jnp.concatenate(turned, 0), tables_ref[2], tables_ref[3])


def gather_rows(rows_ref, channels):
    return jnp.concatenate([rows_ref[pl.ds(c, RADIX, stride=channels), :] for c in range(channels)], 1)


def kernel_spectrum_body(half, kernel_ref, tables_ref, out_ref, rows_ref):
    channels = kernel_ref.shape[0]
    for a in range(RADIX):
        row = ((a % half) * (RADIX // half) + a // half) * channels
        rows_ref[row : row + channels, :] = kernel_ref[:, a * RADIX : (a + 1) * RADIX]
    high, low = halves(gather_rows(rows_ref, channels))
    first_hi, first_lo = tables_ref[0, :, :RADIX], tables_ref[0, :, RADIX:]
    step = mm(first_hi, high) + mm(first_hi, low) + mm(first_lo, high)
    out_ref[...] = spectrum(step, tables_ref)


def channel_rows(signal_ref, count, h):
    return jnp.concatenate(
        [signal_ref[:, :, i * count + h * RADIX : i * count + (h + 1) * RADIX].astype(F32) for i in range(SIDE)], 1
    )


def first_tokens(signal_ref, taps_ref, count):
    own = signal_ref[:, :, SIDE * count :].astype(F32)
    own = jnp.concatenate([own] + [jnp.roll(own, -i * (RADIX // SIDE), 2) for i in range(1, SIDE)], 1)
    head = channel_rows(signal_ref, count, 0)
    previous = jnp.concatenate([jnp.zeros_like(own[:1]), own[:-1]], 0)
    sources, channels = own.shape[:2]
    own, previous, head = (x.reshape(sources * channels, RADIX) for x in (own, previous, head))
    lane = lax.broadcasted_iota(jnp.int32, own.shape, 1)
    window = jnp.where(lane < 16, previous, pltpu.roll(own, 16, 1))
    total = jnp.zeros_like(window)
    for j in range(TAPS):
        tap = jnp.broadcast_to(taps_ref[:, j : j + 1], (channels, RADIX))[None]
        tap = jnp.broadcast_to(tap, (sources, channels, RADIX)).reshape(window.shape)
        total = total + tap * (pltpu.roll(window, j, 1) if j else window)
    return jnp.where(lane < 8, pltpu.roll(total * own, RADIX - 16, 1), head)


def filter_body(signal_ref, taps_ref, spec_ref, tables_ref, out_ref, rows_ref, back_ref):
    sources, channels, count = out_ref.shape
    half = count // RADIX
    rows = sources * channels
    rows_ref[:rows, :] = first_tokens(signal_ref, taps_ref, count)
    for h in range(1, half):
        part = channel_rows(signal_ref, count, h)
        rows_ref[h * rows : (h + 1) * rows, :] = part.reshape(rows, RADIX)
    data = gather_rows(rows_ref, channels).astype(BF16)
    step = mm(tables_ref[0], jnp.concatenate([data, data], 0))
    both = spectrum(step, tables_ref)
    sig_r, sig_i = both[:, :RADIX], both[:, RADIX:]
    ker_r, ker_i = spec_ref[:, :RADIX], spec_ref[:, RADIX:]
    both = jnp.concatenate([sig_r * ker_r - sig_i * ker_i, sig_r * ker_i + sig_i * ker_r], 1)
    both = product3(both, tables_ref[4], tables_ref[5])
    cos, sin = twists(tables_ref)
    turned = []
    for c in range(channels):
        lines = slice(c * RADIX, (c + 1) * RADIX)
        real, imag = both[lines, :RADIX], both[lines, RADIX:]
        turned.append(jnp.concatenate([real * cos - imag * sin, imag * cos + real * sin], 0))
    high, low = halves(jnp.concatenate(turned, 1))
    last_hi, last_lo = tables_ref[1, :RADIX], tables_ref[1, RADIX:]
    result = mm(last_hi, high) + mm(last_hi, low) + mm(last_lo, high)
    for c in range(channels):
        back_ref[pl.ds(c, RADIX, stride=channels), :] = result[:, c * RADIX : (c + 1) * RADIX]
    for h in range(half):
        part = back_ref[h * rows : (h + 1) * rows, :].astype(BF16)
        out_ref[:, :, h * RADIX : (h + 1) * RADIX] = part.reshape(sources, channels, RADIX)


def attention_body(block_ref, query_ref, key_ref, value_ref, one_ref, two_ref, three_ref, out_ref, sum_ref):
    count, width = query_ref.shape
    block = block_ref[0]
    earlier = (three_ref, two_ref, one_ref)
    row = lax.broadcasted_iota(jnp.int32, (count, count), 0)
    col = lax.broadcasted_iota(jnp.int32, (count, count), 1)
    causal = col <= row
    squares = jnp.zeros((count, HD), F32)
    for h in range(width // HD):
        lanes = slice(h * HD, (h + 1) * HD)
        query = query_ref[:, lanes]
        keys = jnp.concatenate([ref[0:count, lanes] for ref in earlier] + [key_ref[:, lanes]], 0)
        values = jnp.concatenate([ref[count:, lanes] for ref in earlier] + [value_ref[:, lanes]], 0)
        scores = lax.dot_general(query, keys, (((1,), (1,)), ((), ())), preferred_element_type=F32) * (
            1.0 / math.sqrt(HD)
        )
        parts = []
        for i in range(SPAN):
            seen = scores[:, i * count : (i + 1) * count]
            parts.append(jnp.where(block >= SPAN - i, seen, -1e30))
        parts.append(jnp.where(causal, scores[:, SPAN * count :], -1e30))
        scores = jnp.concatenate(parts, 1)
        top = jnp.max(scores, axis=1, keepdims=True)
        probs = jnp.exp(scores - top)
        total = jnp.sum(probs, axis=1, keepdims=True)
        numer = mm(probs.astype(BF16), values)
        branch = numer / total
        out_ref[:, lanes] = branch
        squares = squares + branch * branch
    sum_ref[...] = squares.T


def attend(block, query, key, value, one, two, three):
    count, width = query.shape
    vmem = pl.BlockSpec(memory_space=pltpu.VMEM)
    return pl.pallas_call(
        attention_body,
        out_shape=(jax.ShapeDtypeStruct((count, width), F32), jax.ShapeDtypeStruct((HD, count), F32)),
        in_specs=[pl.BlockSpec(memory_space=pltpu.SMEM)] + [vmem] * 6,
        out_specs=(vmem, vmem),
        compiler_params=pltpu.CompilerParams(vmem_limit_bytes=VMEM_LIMIT),
        name="attention",
    )(block, query, key, value, one, two, three)


def sums_body(returned_ref, query_t_ref, att_ref, out_ref):
    mixed = returned_ref[...].astype(F32).reshape(query_t_ref.shape) * query_t_ref[...].astype(F32)
    mixer = jnp.sum(mixed * mixed, axis=0, keepdims=True)
    attention = jnp.sum(att_ref[...], axis=0, keepdims=True)
    rows = jnp.concatenate(
        [attention[:, :RADIX], attention[:, RADIX:], mixer[:, :RADIX], mixer[:, RADIX:], jnp.zeros((4, RADIX), F32)], 0
    )
    out_ref[...] = jnp.broadcast_to(rows[None], out_ref.shape)


def mixed_body(returned_ref, query_ref, beta_ref, out_ref):
    count, width = query_ref.shape
    returned = returned_ref[...].astype(F32).reshape(width, count).T
    out_ref[...] = query_ref[...].astype(F32) * returned * beta_ref[...]


def join_body(sums_ref, att_ref, mixed_ref, beta_ref, out_ref):
    count, _ = att_ref.shape
    total = sums_ref[0]
    for peer in range(1, sums_ref.shape[0]):
        total = total + sums_ref[peer]
    scale = lax.rsqrt(total * (1.0 / D) + 1e-05) * 0.5
    columns = jnp.concatenate([scale, jnp.zeros((RADIX - 8, RADIX), F32)], 0).T
    for h in range(count // RADIX):
        rows = slice(h * RADIX, (h + 1) * RADIX)
        attention_scale = columns[:, h : h + 1]
        mixer_scale = columns[:, 2 + h : 3 + h]
        out_ref[rows, :] = (
            beta_ref[...] * att_ref[rows, :] * attention_scale + mixed_ref[rows, :] * mixer_scale
        ).astype(BF16)


def transpose_body(in_ref, out_ref):
    out_ref[...] = in_ref[...].astype(F32).T.astype(BF16)


def mixer(
    mixer_query,
    mixer_key,
    mixer_value,
    shift_taps,
    conv_kernel,
    heads_query,
    heads_key,
    heads_value,
    beta_attention,
    beta_mixer,
):
    count, width = mixer_key.shape
    blocks = lax.axis_size("seq")
    peers = lax.axis_size("head")
    channels = width // blocks
    sds = jax.ShapeDtypeStruct
    tables = conv_tables(count)
    onward = [(i, i + 1) for i in range(blocks - 1)]
    seq = lax.axis_index("seq")

    signal = kernel_call(
        shift_body, sds((blocks, channels // SIDE, SIDE * count + RADIX), BF16), [pltpu.VMEM((count + 8, width), F32)]
    )(mixer_key, mixer_value, shift_taps)
    received = lax.all_to_all(signal, "seq", 0, 0, tiled=True)
    own_taps = lax.dynamic_slice(shift_taps, (0, seq * channels), (TAPS, channels)).T
    rows = pltpu.VMEM((channels * RADIX, RADIX), F32)
    kernel_spectrum = kernel_call(
        functools.partial(kernel_spectrum_body, count // RADIX), sds((channels * RADIX, 2 * RADIX), F32), [rows]
    )(conv_kernel, tables)
    filtered = kernel_call(
        filter_body, sds((blocks, channels, count), BF16), [rows, rows]
    )(received, own_taps, kernel_spectrum, tables)
    returned = lax.all_to_all(filtered, "seq", 0, 0, tiled=True)

    own = jnp.concatenate([heads_key, heads_value], 0)
    two_back = lax.ppermute(own, "seq", [(i, i + 2) for i in range(blocks - 2)])
    one_back = lax.ppermute(
        jnp.where(seq % 2 == 1, two_back, own), "seq", [(i, i ^ 1) for i in range(blocks)]
    )
    three_back = lax.ppermute(two_back, "seq", onward)
    block = seq.astype(jnp.int32).reshape(1)
    attention_branch, attention_squares = attend(block, heads_query, heads_key, heads_value, one_back, two_back, three_back)
    query_t = kernel_call(transpose_body, sds((width, count), BF16))(mixer_query)
    sums = kernel_call(sums_body, sds((peers, 8, RADIX), F32))(returned, query_t, attention_squares)
    gathered = lax.all_to_all(sums, "head", 0, 0, tiled=True)
    mixed = kernel_call(mixed_body, sds((count, width), F32))(
        returned, mixer_query, beta_mixer[None, :]
    )
    return kernel_call(join_body, sds((count, width), BF16))(gathered, attention_branch, mixed, beta_attention[None, :])


def solution(mesh):
    return jax.shard_map(
        mixer,
        mesh=mesh,
        in_specs=(
            P("seq", "head"),
            P("seq", "head"),
            P("seq", "head"),
            P(None, "head"),
            P(("head", "seq"), None),
            P("seq", "head"),
            P("seq", "head"),
            P("seq", "head"),
            P("head"),
            P("head"),
        ),
        out_specs=P("seq", "head"),
        check_vma=False,
    )
```

```python
import functools
import math

import jax
import jax.numpy as jnp
import numpy as np
from jax import lax
from jax.experimental import pallas as pl
from jax.experimental.pallas import tpu as pltpu
from jax.sharding import PartitionSpec as P


D = 4096
HD = 128
TAPS = 8
SPAN = 3
SIDE = 4
RADIX = 128
VMEM_LIMIT = 20 * 2**20
F32 = jnp.float32
BF16 = jnp.bfloat16


def split_table(table):
    high = table.astype(np.float32).astype(jnp.bfloat16)
    low = (table - high.astype(np.float64)).astype(np.float32).astype(jnp.bfloat16)
    return high, low


def conv_tables(tokens):
    half = tokens // RADIX
    place = np.arange(RADIX)
    order = (place % (RADIX // half)) * half + place // (RADIX // half)
    freq = np.arange(RADIX) + 0.5
    one = 2.0 * np.pi * np.outer(freq, order) / (2 * RADIX)
    first = np.concatenate([np.cos(one), -np.sin(one)], 0)
    last = first.T * (1.0 / (RADIX * RADIX))
    twist = 2.0 * np.pi * np.outer(freq, place) / (2 * RADIX * RADIX)
    two = 2.0 * np.pi * np.outer(place, place) / RADIX
    cos, sin = np.cos(two), np.sin(two)
    ahead = np.block([[cos, -sin], [sin, cos]])
    back = np.block([[cos, sin], [-sin, cos]])
    products = [
        np.concatenate(split_table(first), 1),
        np.concatenate(split_table(last), 0),
        *split_table(ahead),
        *split_table(back),
        np.concatenate(split_table(np.concatenate([np.cos(twist), np.sin(twist)], 1)), 0),
    ]
    return jnp.asarray(np.stack(products))


def halves(value):
    high = value.astype(BF16)
    return high, (value - high.astype(F32)).astype(BF16)


def mm(left, right):
    return lax.dot_general(left, right, (((1,), (0,)), ((), ())), preferred_element_type=F32)


def kernel_call(body, out_shape, scratch=()):
    def call(*args):
        return pl.pallas_call(
            body,
            out_shape=out_shape,
            scratch_shapes=list(scratch),
            compiler_params=pltpu.CompilerParams(vmem_limit_bytes=VMEM_LIMIT),
        )(*args)

    return call


def shift_body(key_ref, value_ref, taps_ref, out_ref, ext_ref):
    count, width = key_ref.shape
    ext_ref[0:8, :] = jnp.zeros((8, width), F32)
    ext_ref[8 : 8 + count, :] = key_ref[...].astype(F32)
    taps = taps_ref[...]
    total = taps[0:1, :] * ext_ref[8 : 8 + count, :]
    for j in range(1, TAPS):
        total = total + taps[j : j + 1, :] * ext_ref[8 - j : 8 - j + count, :]
    product = total * value_ref[...].astype(F32)
    edges = jnp.concatenate(
        [
            ext_ref[8:16, :],
            ext_ref[count : 8 + count, :],
            value_ref[0:16, :].astype(F32)[0:8],
            jnp.zeros((RADIX - 24, width), F32),
        ],
        0,
    )
    blocks, lines = out_ref.shape[:2]
    product = product.T.reshape(blocks, SIDE, lines, count)
    edges = edges.T.reshape(blocks, SIDE, lines, RADIX)
    for i in range(SIDE):
        out_ref[:, :, i * count : (i + 1) * count] = product[:, i].astype(BF16)
    joined = jnp.concatenate([edges[:, i, :, : RADIX // SIDE] for i in range(SIDE)], 2)
    out_ref[:, :, SIDE * count :] = joined.astype(BF16)


def product3(value, table_hi, table_lo):
    high, low = halves(value)
    return mm(high, table_hi) + mm(low, table_hi) + mm(high, table_lo)


def twists(tables_ref):
    table = tables_ref[6].astype(F32)
    table = table[:RADIX] + table[RADIX:]
    return table[:, :RADIX], table[:, RADIX:]


def spectrum(step, tables_ref):
    cos, sin = twists(tables_ref)
    turned = []
    for c in range(step.shape[1] // RADIX):
        lanes = slice(c * RADIX, (c + 1) * RADIX)
        real, imag = step[:RADIX, lanes], step[RADIX:, lanes]
        turned.append(jnp.concatenate([real * cos + imag * sin, imag * cos - real * sin], 1))
    return product3(jnp.concatenate(turned, 0), tables_ref[2], tables_ref[3])


def gather_rows(rows_ref, channels):
    return jnp.concatenate([rows_ref[pl.ds(c, RADIX, stride=channels), :] for c in range(channels)], 1)


def kernel_spectrum_body(half, kernel_ref, tables_ref, out_ref, rows_ref):
    channels = kernel_ref.shape[0]
    for a in range(RADIX):
        row = ((a % half) * (RADIX // half) + a // half) * channels
        rows_ref[row : row + channels, :] = kernel_ref[:, a * RADIX : (a + 1) * RADIX]
    high, low = halves(gather_rows(rows_ref, channels))
    step = mm(tables_ref[0], jnp.concatenate([high, high], 0)) + mm(tables_ref[0, :, :RADIX], low)
    out_ref[...] = spectrum(step, tables_ref)


def channel_rows(signal_ref, count, h):
    return jnp.concatenate(
        [signal_ref[:, :, i * count + h * RADIX : i * count + (h + 1) * RADIX].astype(F32) for i in range(SIDE)], 1
    )


def first_tokens(signal_ref, taps_ref, count):
    own = signal_ref[:, :, SIDE * count :].astype(F32)
    own = jnp.concatenate([own] + [jnp.roll(own, -i * (RADIX // SIDE), 2) for i in range(1, SIDE)], 1)
    head = channel_rows(signal_ref, count, 0)
    previous = jnp.concatenate([jnp.zeros_like(own[:1]), own[:-1]], 0)
    sources, channels = own.shape[:2]
    own, previous, head = (x.reshape(sources * channels, RADIX) for x in (own, previous, head))
    lane = lax.broadcasted_iota(jnp.int32, own.shape, 1)
    window = jnp.where(lane < 16, previous, pltpu.roll(own, 16, 1))
    total = jnp.zeros_like(window)
    for j in range(TAPS):
        tap = jnp.broadcast_to(taps_ref[:, j : j + 1], (channels, RADIX))[None]
        tap = jnp.broadcast_to(tap, (sources, channels, RADIX)).reshape(window.shape)
        total = total + tap * (pltpu.roll(window, j, 1) if j else window)
    return jnp.where(lane < 8, pltpu.roll(total * own, RADIX - 16, 1), head)


def filter_body(signal_ref, taps_ref, spec_ref, tables_ref, out_ref, rows_ref, back_ref):
    sources, channels, count = out_ref.shape
    half = count // RADIX
    rows = sources * channels
    rows_ref[:rows, :] = first_tokens(signal_ref, taps_ref, count)
    for h in range(1, half):
        part = channel_rows(signal_ref, count, h)
        rows_ref[h * rows : (h + 1) * rows, :] = part.reshape(rows, RADIX)
    data = gather_rows(rows_ref, channels).astype(BF16)
    step = mm(tables_ref[0], jnp.concatenate([data, data], 0))
    both = spectrum(step, tables_ref)
    sig_r, sig_i = both[:, :RADIX], both[:, RADIX:]
    ker_r, ker_i = spec_ref[:, :RADIX], spec_ref[:, RADIX:]
    both = jnp.concatenate([sig_r * ker_r - sig_i * ker_i, sig_r * ker_i + sig_i * ker_r], 1)
    both = product3(both, tables_ref[4], tables_ref[5])
    cos, sin = twists(tables_ref)
    turned = []
    for c in range(channels):
        lines = slice(c * RADIX, (c + 1) * RADIX)
        real, imag = both[lines, :RADIX], both[lines, RADIX:]
        turned.append(jnp.concatenate([real * cos - imag * sin, imag * cos + real * sin], 0))
    high, low = halves(jnp.concatenate(turned, 1))
    both = mm(tables_ref[1], high)
    result = both[:RADIX] + both[RADIX:] + mm(tables_ref[1, :RADIX], low)
    for c in range(channels):
        back_ref[pl.ds(c, RADIX, stride=channels), :] = result[:, c * RADIX : (c + 1) * RADIX]
    for h in range(half):
        part = back_ref[h * rows : (h + 1) * rows, :].astype(BF16)
        out_ref[:, :, h * RADIX : (h + 1) * RADIX] = part.reshape(sources, channels, RADIX)


def attention_body(block_ref, query_ref, key_ref, value_ref, one_ref, two_ref, three_ref, out_ref, sum_ref):
    count, width = query_ref.shape
    block = block_ref[0]
    earlier = (three_ref, two_ref, one_ref)
    row = lax.broadcasted_iota(jnp.int32, (count, count), 0)
    col = lax.broadcasted_iota(jnp.int32, (count, count), 1)
    causal = col <= row
    squares = jnp.zeros((count, HD), F32)
    for h in range(width // HD):
        lanes = slice(h * HD, (h + 1) * HD)
        query = query_ref[:, lanes]
        keys = jnp.concatenate([ref[0:count, lanes] for ref in earlier] + [key_ref[:, lanes]], 0)
        values = jnp.concatenate([ref[count:, lanes] for ref in earlier] + [value_ref[:, lanes]], 0)
        scores = lax.dot_general(query, keys, (((1,), (1,)), ((), ())), preferred_element_type=F32) * (
            1.0 / math.sqrt(HD)
        )
        parts = []
        for i in range(SPAN):
            seen = scores[:, i * count : (i + 1) * count]
            parts.append(jnp.where(block >= SPAN - i, seen, -1e30))
        parts.append(jnp.where(causal, scores[:, SPAN * count :], -1e30))
        scores = jnp.concatenate(parts, 1)
        top = jnp.max(scores, axis=1, keepdims=True)
        probs = jnp.exp(scores - top)
        total = jnp.sum(probs, axis=1, keepdims=True)
        numer = mm(probs.astype(BF16), values)
        branch = numer / total
        out_ref[:, lanes] = branch
        squares = squares + branch * branch
    sum_ref[...] = squares.T


def attend(block, query, key, value, one, two, three):
    count, width = query.shape
    vmem = pl.BlockSpec(memory_space=pltpu.VMEM)
    return pl.pallas_call(
        attention_body,
        out_shape=(jax.ShapeDtypeStruct((count, width), F32), jax.ShapeDtypeStruct((HD, count), F32)),
        in_specs=[pl.BlockSpec(memory_space=pltpu.SMEM)] + [vmem] * 6,
        out_specs=(vmem, vmem),
        compiler_params=pltpu.CompilerParams(vmem_limit_bytes=VMEM_LIMIT),
        name="attention",
    )(block, query, key, value, one, two, three)


def sums_body(returned_ref, query_t_ref, att_ref, out_ref):
    mixed = returned_ref[...].astype(F32).reshape(query_t_ref.shape) * query_t_ref[...].astype(F32)
    mixer = jnp.sum(mixed * mixed, axis=0, keepdims=True)
    attention = jnp.sum(att_ref[...], axis=0, keepdims=True)
    rows = jnp.concatenate(
        [attention[:, :RADIX], attention[:, RADIX:], mixer[:, :RADIX], mixer[:, RADIX:], jnp.zeros((4, RADIX), F32)], 0
    )
    out_ref[...] = jnp.broadcast_to(rows[None], out_ref.shape)


def mixed_body(returned_ref, query_ref, beta_ref, out_ref):
    count, width = query_ref.shape
    returned = returned_ref[...].astype(F32).reshape(width, count).T
    out_ref[...] = query_ref[...].astype(F32) * returned * beta_ref[...]


def join_body(sums_ref, att_ref, mixed_ref, beta_ref, out_ref):
    count, _ = att_ref.shape
    total = sums_ref[0]
    for peer in range(1, sums_ref.shape[0]):
        total = total + sums_ref[peer]
    scale = lax.rsqrt(total * (1.0 / D) + 1e-05) * 0.5
    columns = jnp.concatenate([scale, jnp.zeros((RADIX - 8, RADIX), F32)], 0).T
    for h in range(count // RADIX):
        rows = slice(h * RADIX, (h + 1) * RADIX)
        attention_scale = columns[:, h : h + 1]
        mixer_scale = columns[:, 2 + h : 3 + h]
        out_ref[rows, :] = (
            beta_ref[...] * att_ref[rows, :] * attention_scale + mixed_ref[rows, :] * mixer_scale
        ).astype(BF16)


def transpose_body(in_ref, out_ref):
    out_ref[...] = in_ref[...].astype(F32).T.astype(BF16)


def mixer(
    mixer_query,
    mixer_key,
    mixer_value,
    shift_taps,
    conv_kernel,
    heads_query,
    heads_key,
    heads_value,
    beta_attention,
    beta_mixer,
):
    count, width = mixer_key.shape
    blocks = lax.axis_size("seq")
    peers = lax.axis_size("head")
    channels = width // blocks
    sds = jax.ShapeDtypeStruct
    tables = conv_tables(count)
    onward = [(i, i + 1) for i in range(blocks - 1)]
    seq = lax.axis_index("seq")

    signal = kernel_call(
        shift_body, sds((blocks, channels // SIDE, SIDE * count + RADIX), BF16), [pltpu.VMEM((count + 8, width), F32)]
    )(mixer_key, mixer_value, shift_taps)
    received = lax.all_to_all(signal, "seq", 0, 0, tiled=True)
    own_taps = lax.dynamic_slice(shift_taps, (0, seq * channels), (TAPS, channels)).T
    rows = pltpu.VMEM((channels * RADIX, RADIX), F32)
    kernel_spectrum = kernel_call(
        functools.partial(kernel_spectrum_body, count // RADIX), sds((channels * RADIX, 2 * RADIX), F32), [rows]
    )(conv_kernel, tables)
    filtered = kernel_call(
        filter_body, sds((blocks, channels, count), BF16), [rows, rows]
    )(received, own_taps, kernel_spectrum, tables)
    returned = lax.all_to_all(filtered, "seq", 0, 0, tiled=True)

    own = jnp.concatenate([heads_key, heads_value], 0)
    two_back = lax.ppermute(own, "seq", [(i, i + 2) for i in range(blocks - 2)])
    three_back = lax.ppermute(two_back, "seq", onward)
    two_back, three_back = lax.optimization_barrier((two_back, three_back))
    odd = seq % 2 == 1
    exchanged = jnp.concatenate(
        [jnp.where(odd, two_back[:count], heads_key), jnp.where(odd, two_back[count:], heads_value)], 0
    )
    one_back = lax.ppermute(exchanged, "seq", [(i, i ^ 1) for i in range(blocks)])
    block = seq.astype(jnp.int32).reshape(1)
    attention_branch, attention_squares = attend(block, heads_query, heads_key, heads_value, one_back, two_back, three_back)
    query_t = kernel_call(transpose_body, sds((width, count), BF16))(mixer_query)
    sums = kernel_call(sums_body, sds((peers, 8, RADIX), F32))(returned, query_t, attention_squares)
    gathered = lax.all_to_all(sums, "head", 0, 0, tiled=True)
    mixed = kernel_call(mixed_body, sds((count, width), F32))(
        returned, mixer_query, beta_mixer[None, :]
    )
    return kernel_call(join_body, sds((count, width), BF16))(gathered, attention_branch, mixed, beta_attention[None, :])


def solution(mesh):
    return jax.shard_map(
        mixer,
        mesh=mesh,
        in_specs=(
            P("seq", "head"),
            P("seq", "head"),
            P("seq", "head"),
            P(None, "head"),
            P(("head", "seq"), None),
            P("seq", "head"),
            P("seq", "head"),
            P("seq", "head"),
            P("head"),
            P("head"),
        ),
        out_specs=P("seq", "head"),
        check_vma=False,
    )
```

```python
import functools
import math

import jax
import jax.numpy as jnp
import numpy as np
from jax import lax
from jax.experimental import pallas as pl
from jax.experimental.pallas import tpu as pltpu
from jax.sharding import PartitionSpec as P


D = 4096
HD = 128
TAPS = 8
SPAN = 3
SIDE = 4
RADIX = 128
VMEM_LIMIT = 20 * 2**20
F32 = jnp.float32
BF16 = jnp.bfloat16


def split_table(table):
    high = table.astype(np.float32).astype(jnp.bfloat16)
    low = (table - high.astype(np.float64)).astype(np.float32).astype(jnp.bfloat16)
    return high, low


def conv_tables(tokens):
    half = tokens // RADIX
    place = np.arange(RADIX)
    order = (place % (RADIX // half)) * half + place // (RADIX // half)
    freq = np.arange(RADIX) + 0.5
    one = 2.0 * np.pi * np.outer(freq, order) / (2 * RADIX)
    first = np.concatenate([np.cos(one), -np.sin(one)], 0)
    last = first.T * (1.0 / (RADIX * RADIX))
    twist = 2.0 * np.pi * np.outer(freq, place) / (2 * RADIX * RADIX)
    two = 2.0 * np.pi * np.outer(place, place) / RADIX
    cos, sin = np.cos(two), np.sin(two)
    ahead = np.block([[cos, -sin], [sin, cos]])
    back = np.block([[cos, sin], [-sin, cos]])
    products = [
        np.concatenate(split_table(first), 1),
        np.concatenate(split_table(last), 0),
        *split_table(ahead),
        *split_table(back),
        np.concatenate(split_table(np.concatenate([np.cos(twist), np.sin(twist)], 1)), 0),
    ]
    return jnp.asarray(np.stack(products))


def halves(value):
    high = value.astype(BF16)
    return high, (value - high.astype(F32)).astype(BF16)


def mm(left, right):
    return lax.dot_general(left, right, (((1,), (0,)), ((), ())), preferred_element_type=F32)


def kernel_call(body, out_shape, scratch=()):
    def call(*args):
        return pl.pallas_call(
            body,
            out_shape=out_shape,
            scratch_shapes=list(scratch),
            compiler_params=pltpu.CompilerParams(vmem_limit_bytes=VMEM_LIMIT),
        )(*args)

    return call


def shift_body(key_ref, value_ref, taps_ref, out_ref, ext_ref):
    count, width = key_ref.shape
    ext_ref[0:8, :] = jnp.zeros((8, width), F32)
    ext_ref[8 : 8 + count, :] = key_ref[...].astype(F32)
    taps = taps_ref[...]
    total = taps[0:1, :] * ext_ref[8 : 8 + count, :]
    for j in range(1, TAPS):
        total = total + taps[j : j + 1, :] * ext_ref[8 - j : 8 - j + count, :]
    product = total * value_ref[...].astype(F32)
    edges = jnp.concatenate(
        [
            ext_ref[8:16, :],
            ext_ref[count : 8 + count, :],
            value_ref[0:16, :].astype(F32)[0:8],
            jnp.zeros((RADIX - 24, width), F32),
        ],
        0,
    )
    blocks, lines = out_ref.shape[:2]
    product = product.T.reshape(blocks, SIDE, lines, count)
    edges = edges.T.reshape(blocks, SIDE, lines, RADIX)
    for i in range(SIDE):
        out_ref[:, :, i * count : (i + 1) * count] = product[:, i].astype(BF16)
    joined = jnp.concatenate([edges[:, i, :, : RADIX // SIDE] for i in range(SIDE)], 2)
    out_ref[:, :, SIDE * count :] = joined.astype(BF16)


def product3(value, table_hi, table_lo):
    high, low = halves(value)
    return mm(high, table_hi) + mm(low, table_hi) + mm(high, table_lo)


def twists(tables_ref):
    table = tables_ref[6].astype(F32)
    table = table[:RADIX] + table[RADIX:]
    return table[:, :RADIX], table[:, RADIX:]


def spectrum(step, tables_ref):
    cos, sin = twists(tables_ref)
    turned = []
    for c in range(step.shape[1] // RADIX):
        lanes = slice(c * RADIX, (c + 1) * RADIX)
        real, imag = step[:RADIX, lanes], step[RADIX:, lanes]
        turned.append(jnp.concatenate([real * cos + imag * sin, imag * cos - real * sin], 1))
    return product3(jnp.concatenate(turned, 0), tables_ref[2], tables_ref[3])


def gather_rows(rows_ref, channels):
    return jnp.concatenate([rows_ref[pl.ds(c, RADIX, stride=channels), :] for c in range(channels)], 1)


def kernel_spectrum_body(half, kernel_in, tables_ref, out_ref, rows_ref, kernel_ref, sem):
    channels = kernel_ref.shape[0]
    copy = pltpu.make_async_copy(kernel_in, kernel_ref, sem)
    copy.start()
    copy.wait()
    for a in range(RADIX):
        row = ((a % half) * (RADIX // half) + a // half) * channels
        rows_ref[row : row + channels, :] = kernel_ref[:, a * RADIX : (a + 1) * RADIX]
    high, low = halves(gather_rows(rows_ref, channels))
    step = mm(tables_ref[0], jnp.concatenate([high, high], 0)) + mm(tables_ref[0, :, :RADIX], low)
    out_ref[...] = spectrum(step, tables_ref)


def channel_rows(signal_ref, count, h):
    return jnp.concatenate(
        [signal_ref[:, :, i * count + h * RADIX : i * count + (h + 1) * RADIX].astype(F32) for i in range(SIDE)], 1
    )


def first_tokens(signal_ref, taps_ref, count):
    own = signal_ref[:, :, SIDE * count :].astype(F32)
    own = jnp.concatenate([own] + [jnp.roll(own, -i * (RADIX // SIDE), 2) for i in range(1, SIDE)], 1)
    head = channel_rows(signal_ref, count, 0)
    previous = jnp.concatenate([jnp.zeros_like(own[:1]), own[:-1]], 0)
    sources, channels = own.shape[:2]
    own, previous, head = (x.reshape(sources * channels, RADIX) for x in (own, previous, head))
    lane = lax.broadcasted_iota(jnp.int32, own.shape, 1)
    window = jnp.where(lane < 16, previous, pltpu.roll(own, 16, 1))
    total = jnp.zeros_like(window)
    for j in range(TAPS):
        tap = jnp.broadcast_to(taps_ref[:, j : j + 1], (channels, RADIX))[None]
        tap = jnp.broadcast_to(tap, (sources, channels, RADIX)).reshape(window.shape)
        total = total + tap * (pltpu.roll(window, j, 1) if j else window)
    return jnp.where(lane < 8, pltpu.roll(total * own, RADIX - 16, 1), head)


def filter_body(signal_ref, taps_ref, spec_ref, tables_ref, out_ref, rows_ref, back_ref):
    sources, channels, count = out_ref.shape
    half = count // RADIX
    rows = sources * channels
    rows_ref[:rows, :] = first_tokens(signal_ref, taps_ref, count)
    for h in range(1, half):
        part = channel_rows(signal_ref, count, h)
        rows_ref[h * rows : (h + 1) * rows, :] = part.reshape(rows, RADIX)
    data = gather_rows(rows_ref, channels).astype(BF16)
    step = mm(tables_ref[0], jnp.concatenate([data, data], 0))
    both = spectrum(step, tables_ref)
    sig_r, sig_i = both[:, :RADIX], both[:, RADIX:]
    ker_r, ker_i = spec_ref[:, :RADIX], spec_ref[:, RADIX:]
    both = jnp.concatenate([sig_r * ker_r - sig_i * ker_i, sig_r * ker_i + sig_i * ker_r], 1)
    both = product3(both, tables_ref[4], tables_ref[5])
    cos, sin = twists(tables_ref)
    turned = []
    for c in range(channels):
        lines = slice(c * RADIX, (c + 1) * RADIX)
        real, imag = both[lines, :RADIX], both[lines, RADIX:]
        turned.append(jnp.concatenate([real * cos - imag * sin, imag * cos + real * sin], 0))
    high, low = halves(jnp.concatenate(turned, 1))
    both = mm(tables_ref[1], high)
    result = both[:RADIX] + both[RADIX:] + mm(tables_ref[1, :RADIX], low)
    for c in range(channels):
        back_ref[pl.ds(c, RADIX, stride=channels), :] = result[:, c * RADIX : (c + 1) * RADIX]
    for h in range(half):
        part = back_ref[h * rows : (h + 1) * rows, :].astype(BF16)
        out_ref[:, :, h * RADIX : (h + 1) * RADIX] = part.reshape(sources, channels, RADIX)


def attention_body(block_ref, query_ref, key_ref, value_ref, one_ref, two_ref, three_ref, out_ref, sum_ref):
    count, width = query_ref.shape
    block = block_ref[0]
    earlier = (three_ref, two_ref, one_ref)
    row = lax.broadcasted_iota(jnp.int32, (count, count), 0)
    col = lax.broadcasted_iota(jnp.int32, (count, count), 1)
    causal = col <= row
    squares = jnp.zeros((count, HD), F32)
    for h in range(width // HD):
        lanes = slice(h * HD, (h + 1) * HD)
        query = query_ref[:, lanes]
        keys = jnp.concatenate([ref[0:count, lanes] for ref in earlier] + [key_ref[:, lanes]], 0)
        values = jnp.concatenate([ref[count:, lanes] for ref in earlier] + [value_ref[:, lanes]], 0)
        scores = lax.dot_general(query, keys, (((1,), (1,)), ((), ())), preferred_element_type=F32) * (
            1.0 / math.sqrt(HD)
        )
        parts = []
        for i in range(SPAN):
            seen = scores[:, i * count : (i + 1) * count]
            parts.append(jnp.where(block >= SPAN - i, seen, -1e30))
        parts.append(jnp.where(causal, scores[:, SPAN * count :], -1e30))
        scores = jnp.concatenate(parts, 1)
        top = jnp.max(scores, axis=1, keepdims=True)
        probs = jnp.exp(scores - top)
        total = jnp.sum(probs, axis=1, keepdims=True)
        numer = mm(probs.astype(BF16), values)
        branch = numer / total
        out_ref[:, lanes] = branch
        squares = squares + branch * branch
    sum_ref[...] = squares.T


def attend(block, query, key, value, one, two, three):
    count, width = query.shape
    vmem = pl.BlockSpec(memory_space=pltpu.VMEM)
    return pl.pallas_call(
        attention_body,
        out_shape=(jax.ShapeDtypeStruct((count, width), F32), jax.ShapeDtypeStruct((HD, count), F32)),
        in_specs=[pl.BlockSpec(memory_space=pltpu.SMEM)] + [vmem] * 6,
        out_specs=(vmem, vmem),
        compiler_params=pltpu.CompilerParams(vmem_limit_bytes=VMEM_LIMIT),
        name="attention",
    )(block, query, key, value, one, two, three)


def sums_body(returned_ref, query_t_ref, att_ref, out_ref):
    mixed = returned_ref[...].astype(F32).reshape(query_t_ref.shape) * query_t_ref[...].astype(F32)
    mixer = jnp.sum(mixed * mixed, axis=0, keepdims=True)
    attention = jnp.sum(att_ref[...], axis=0, keepdims=True)
    rows = jnp.concatenate(
        [attention[:, :RADIX], attention[:, RADIX:], mixer[:, :RADIX], mixer[:, RADIX:], jnp.zeros((4, RADIX), F32)], 0
    )
    out_ref[...] = jnp.broadcast_to(rows[None], out_ref.shape)


def mixed_body(returned_ref, query_ref, beta_ref, out_ref):
    count, width = query_ref.shape
    returned = returned_ref[...].astype(F32).reshape(width, count).T
    out_ref[...] = query_ref[...].astype(F32) * returned * beta_ref[...]


def join_body(sums_ref, att_ref, mixed_ref, beta_ref, out_ref):
    count, _ = att_ref.shape
    total = sums_ref[0]
    for peer in range(1, sums_ref.shape[0]):
        total = total + sums_ref[peer]
    scale = lax.rsqrt(total * (1.0 / D) + 1e-05) * 0.5
    columns = jnp.concatenate([scale, jnp.zeros((RADIX - 8, RADIX), F32)], 0).T
    for h in range(count // RADIX):
        rows = slice(h * RADIX, (h + 1) * RADIX)
        attention_scale = columns[:, h : h + 1]
        mixer_scale = columns[:, 2 + h : 3 + h]
        out_ref[rows, :] = (
            beta_ref[...] * att_ref[rows, :] * attention_scale + mixed_ref[rows, :] * mixer_scale
        ).astype(BF16)


def transpose_body(in_ref, out_ref):
    out_ref[...] = in_ref[...].astype(F32).T.astype(BF16)


def mixer(
    mixer_query,
    mixer_key,
    mixer_value,
    shift_taps,
    conv_kernel,
    heads_query,
    heads_key,
    heads_value,
    beta_attention,
    beta_mixer,
):
    count, width = mixer_key.shape
    blocks = lax.axis_size("seq")
    peers = lax.axis_size("head")
    channels = width // blocks
    sds = jax.ShapeDtypeStruct
    tables = conv_tables(count)
    onward = [(i, i + 1) for i in range(blocks - 1)]
    seq = lax.axis_index("seq")

    signal = kernel_call(
        shift_body, sds((blocks, channels // SIDE, SIDE * count + RADIX), BF16), [pltpu.VMEM((count + 8, width), F32)]
    )(mixer_key, mixer_value, shift_taps)
    received = lax.all_to_all(signal, "seq", 0, 0, tiled=True)
    own_taps = lax.dynamic_slice(shift_taps, (0, seq * channels), (TAPS, channels)).T
    rows = pltpu.VMEM((channels * RADIX, RADIX), F32)
    kernel_spectrum = pl.pallas_call(
        functools.partial(kernel_spectrum_body, count // RADIX),
        out_shape=sds((channels * RADIX, 2 * RADIX), F32),
        in_specs=[pl.BlockSpec(memory_space=pltpu.HBM), pl.BlockSpec(memory_space=pltpu.VMEM)],
        scratch_shapes=[rows, pltpu.VMEM(conv_kernel.shape, F32), pltpu.SemaphoreType.DMA],
        compiler_params=pltpu.CompilerParams(vmem_limit_bytes=VMEM_LIMIT),
        name="kernel_spectrum",
    )(pltpu.with_memory_space_constraint(conv_kernel, pltpu.HBM), tables)
    filtered = kernel_call(
        filter_body, sds((blocks, channels, count), BF16), [rows, rows]
    )(received, own_taps, kernel_spectrum, tables)
    returned = lax.all_to_all(filtered, "seq", 0, 0, tiled=True)

    own = jnp.concatenate([heads_key, heads_value], 0)
    two_back = lax.ppermute(own, "seq", [(i, i + 2) for i in range(blocks - 2)])
    three_back = lax.ppermute(two_back, "seq", onward)
    two_back, three_back = lax.optimization_barrier((two_back, three_back))
    odd = seq % 2 == 1
    exchanged = jnp.concatenate(
        [jnp.where(odd, two_back[:count], heads_key), jnp.where(odd, two_back[count:], heads_value)], 0
    )
    one_back = lax.ppermute(exchanged, "seq", [(i, i ^ 1) for i in range(blocks)])
    block = seq.astype(jnp.int32).reshape(1)
    attention_branch, attention_squares = attend(block, heads_query, heads_key, heads_value, one_back, two_back, three_back)
    query_t = kernel_call(transpose_body, sds((width, count), BF16))(mixer_query)
    sums = kernel_call(sums_body, sds((peers, 8, RADIX), F32))(returned, query_t, attention_squares)
    gathered = lax.all_to_all(sums, "head", 0, 0, tiled=True)
    mixed = kernel_call(mixed_body, sds((count, width), F32))(
        returned, mixer_query, beta_mixer[None, :]
    )
    return kernel_call(join_body, sds((count, width), BF16))(gathered, attention_branch, mixed, beta_attention[None, :])


def solution(mesh):
    return jax.shard_map(
        mixer,
        mesh=mesh,
        in_specs=(
            P("seq", "head"),
            P("seq", "head"),
            P("seq", "head"),
            P(None, "head"),
            P(("head", "seq"), None),
            P("seq", "head"),
            P("seq", "head"),
            P("seq", "head"),
            P("head"),
            P("head"),
        ),
        out_specs=P("seq", "head"),
        check_vma=False,
    )
```

```python
import functools
import math

import jax
import jax.numpy as jnp
import numpy as np
from jax import lax
from jax.experimental import pallas as pl
from jax.experimental.pallas import tpu as pltpu
from jax.sharding import PartitionSpec as P


D = 4096
HD = 128
TAPS = 8
SPAN = 3
SIDE = 4
RADIX = 128
VMEM_LIMIT = 20 * 2**20
F32 = jnp.float32
BF16 = jnp.bfloat16


def split_table(table):
    high = table.astype(np.float32).astype(jnp.bfloat16)
    low = (table - high.astype(np.float64)).astype(np.float32).astype(jnp.bfloat16)
    return high, low


def conv_tables(tokens):
    half = tokens // RADIX
    place = np.arange(RADIX)
    order = (place % (RADIX // half)) * half + place // (RADIX // half)
    freq = np.arange(RADIX) + 0.5
    one = 2.0 * np.pi * np.outer(freq, order) / (2 * RADIX)
    first = np.concatenate([np.cos(one), -np.sin(one)], 0)
    last = first.T * (1.0 / (RADIX * RADIX))
    twist = 2.0 * np.pi * np.outer(freq, place) / (2 * RADIX * RADIX)
    two = 2.0 * np.pi * np.outer(place, place) / RADIX
    cos, sin = np.cos(two), np.sin(two)
    ahead = np.block([[cos, -sin], [sin, cos]])
    back = np.block([[cos, sin], [-sin, cos]])
    products = [
        np.concatenate(split_table(first), 1),
        np.concatenate(split_table(last), 0),
        *split_table(ahead),
        *split_table(back),
        np.concatenate(split_table(np.concatenate([np.cos(twist), np.sin(twist)], 1)), 0),
    ]
    return jnp.asarray(np.stack(products))


def halves(value):
    high = value.astype(BF16)
    return high, (value - high.astype(F32)).astype(BF16)


def mm(left, right):
    return lax.dot_general(left, right, (((1,), (0,)), ((), ())), preferred_element_type=F32)


def kernel_call(body, out_shape, scratch=()):
    def call(*args):
        return pl.pallas_call(
            body,
            out_shape=out_shape,
            scratch_shapes=list(scratch),
            compiler_params=pltpu.CompilerParams(vmem_limit_bytes=VMEM_LIMIT),
        )(*args)

    return call


def shift_body(key_ref, value_ref, taps_ref, out_ref, ext_ref):
    count, width = key_ref.shape
    ext_ref[0:8, :] = jnp.zeros((8, width), F32)
    ext_ref[8 : 8 + count, :] = key_ref[...].astype(F32)
    taps = taps_ref[...]
    total = taps[0:1, :] * ext_ref[8 : 8 + count, :]
    for j in range(1, TAPS):
        total = total + taps[j : j + 1, :] * ext_ref[8 - j : 8 - j + count, :]
    product = total * value_ref[...].astype(F32)
    edges = jnp.concatenate(
        [
            ext_ref[8:16, :],
            ext_ref[count : 8 + count, :],
            value_ref[0:16, :].astype(F32)[0:8],
            jnp.zeros((RADIX - 24, width), F32),
        ],
        0,
    )
    blocks, lines = out_ref.shape[:2]
    product = product.T.reshape(blocks, SIDE, lines, count)
    edges = edges.T.reshape(blocks, SIDE, lines, RADIX)
    for i in range(SIDE):
        out_ref[:, :, i * count : (i + 1) * count] = product[:, i].astype(BF16)
    joined = jnp.concatenate([edges[:, i, :, : RADIX // SIDE] for i in range(SIDE)], 2)
    out_ref[:, :, SIDE * count :] = joined.astype(BF16)


def pack_body(key_in, value_in, out_ref, sems):
    count = key_in.shape[0]
    copies = [
        pltpu.make_async_copy(source, out_ref.at[pl.ds(i * count, count)], sems.at[i])
        for i, source in enumerate((key_in, value_in))
    ]
    for copy in copies:
        copy.start()
    for copy in copies:
        copy.wait()


def pack(key, value):
    count, width = key.shape
    return pl.pallas_call(
        pack_body,
        out_shape=jax.ShapeDtypeStruct((2 * count, width), key.dtype),
        in_specs=[pl.BlockSpec(memory_space=pltpu.HBM)] * 2,
        out_specs=pl.BlockSpec(memory_space=pltpu.VMEM),
        scratch_shapes=[pltpu.SemaphoreType.DMA((2,))],
        compiler_params=pltpu.CompilerParams(vmem_limit_bytes=VMEM_LIMIT),
        name="pack",
    )(*(pltpu.with_memory_space_constraint(x, pltpu.HBM) for x in (key, value)))


def product3(value, table_hi, table_lo):
    high, low = halves(value)
    return mm(high, table_hi) + mm(low, table_hi) + mm(high, table_lo)


def twists(tables_ref):
    table = tables_ref[6].astype(F32)
    table = table[:RADIX] + table[RADIX:]
    return table[:, :RADIX], table[:, RADIX:]


def spectrum(step, tables_ref):
    cos, sin = twists(tables_ref)
    turned = []
    for c in range(step.shape[1] // RADIX):
        lanes = slice(c * RADIX, (c + 1) * RADIX)
        real, imag = step[:RADIX, lanes], step[RADIX:, lanes]
        turned.append(jnp.concatenate([real * cos + imag * sin, imag * cos - real * sin], 1))
    return product3(jnp.concatenate(turned, 0), tables_ref[2], tables_ref[3])


def gather_rows(rows_ref, channels):
    return jnp.concatenate([rows_ref[pl.ds(c, RADIX, stride=channels), :] for c in range(channels)], 1)


def kernel_spectrum_body(half, kernel_in, tables_ref, out_ref, rows_ref, kernel_ref, sem):
    channels = kernel_ref.shape[0]
    copy = pltpu.make_async_copy(kernel_in, kernel_ref, sem)
    copy.start()
    copy.wait()
    for a in range(RADIX):
        row = ((a % half) * (RADIX // half) + a // half) * channels
        rows_ref[row : row + channels, :] = kernel_ref[:, a * RADIX : (a + 1) * RADIX]
    high, low = halves(gather_rows(rows_ref, channels))
    step = mm(tables_ref[0], jnp.concatenate([high, high], 0)) + mm(tables_ref[0, :, :RADIX], low)
    out_ref[...] = spectrum(step, tables_ref)


def channel_rows(signal_ref, count, h):
    return jnp.concatenate(
        [signal_ref[:, :, i * count + h * RADIX : i * count + (h + 1) * RADIX].astype(F32) for i in range(SIDE)], 1
    )


def first_tokens(signal_ref, taps_ref, count):
    own = signal_ref[:, :, SIDE * count :].astype(F32)
    own = jnp.concatenate([own] + [jnp.roll(own, -i * (RADIX // SIDE), 2) for i in range(1, SIDE)], 1)
    head = channel_rows(signal_ref, count, 0)
    previous = jnp.concatenate([jnp.zeros_like(own[:1]), own[:-1]], 0)
    sources, channels = own.shape[:2]
    own, previous, head = (x.reshape(sources * channels, RADIX) for x in (own, previous, head))
    lane = lax.broadcasted_iota(jnp.int32, own.shape, 1)
    window = jnp.where(lane < 16, previous, pltpu.roll(own, 16, 1))
    total = jnp.zeros_like(window)
    for j in range(TAPS):
        tap = jnp.broadcast_to(taps_ref[:, j : j + 1], (channels, RADIX))[None]
        tap = jnp.broadcast_to(tap, (sources, channels, RADIX)).reshape(window.shape)
        total = total + tap * (pltpu.roll(window, j, 1) if j else window)
    return jnp.where(lane < 8, pltpu.roll(total * own, RADIX - 16, 1), head)


def filter_body(signal_ref, taps_ref, spec_ref, tables_ref, out_ref, rows_ref, back_ref):
    sources, channels, count = out_ref.shape
    half = count // RADIX
    rows = sources * channels
    rows_ref[:rows, :] = first_tokens(signal_ref, taps_ref, count)
    for h in range(1, half):
        part = channel_rows(signal_ref, count, h)
        rows_ref[h * rows : (h + 1) * rows, :] = part.reshape(rows, RADIX)
    data = gather_rows(rows_ref, channels).astype(BF16)
    step = mm(tables_ref[0], jnp.concatenate([data, data], 0))
    both = spectrum(step, tables_ref)
    sig_r, sig_i = both[:, :RADIX], both[:, RADIX:]
    ker_r, ker_i = spec_ref[:, :RADIX], spec_ref[:, RADIX:]
    both = jnp.concatenate([sig_r * ker_r - sig_i * ker_i, sig_r * ker_i + sig_i * ker_r], 1)
    both = product3(both, tables_ref[4], tables_ref[5])
    cos, sin = twists(tables_ref)
    turned = []
    for c in range(channels):
        lines = slice(c * RADIX, (c + 1) * RADIX)
        real, imag = both[lines, :RADIX], both[lines, RADIX:]
        turned.append(jnp.concatenate([real * cos - imag * sin, imag * cos + real * sin], 0))
    high, low = halves(jnp.concatenate(turned, 1))
    both = mm(tables_ref[1], high)
    result = both[:RADIX] + both[RADIX:] + mm(tables_ref[1, :RADIX], low)
    for c in range(channels):
        back_ref[pl.ds(c, RADIX, stride=channels), :] = result[:, c * RADIX : (c + 1) * RADIX]
    for h in range(half):
        part = back_ref[h * rows : (h + 1) * rows, :].astype(BF16)
        out_ref[:, :, h * RADIX : (h + 1) * RADIX] = part.reshape(sources, channels, RADIX)


def attention_body(block_ref, query_ref, key_ref, value_ref, one_ref, two_ref, three_ref, out_ref, sum_ref):
    count, width = query_ref.shape
    block = block_ref[0]
    earlier = (three_ref, two_ref, one_ref)
    row = lax.broadcasted_iota(jnp.int32, (count, count), 0)
    col = lax.broadcasted_iota(jnp.int32, (count, count), 1)
    causal = col <= row
    squares = jnp.zeros((count, HD), F32)
    for h in range(width // HD):
        lanes = slice(h * HD, (h + 1) * HD)
        query = query_ref[:, lanes]
        keys = jnp.concatenate([ref[0:count, lanes] for ref in earlier] + [key_ref[:, lanes]], 0)
        values = jnp.concatenate([ref[count:, lanes] for ref in earlier] + [value_ref[:, lanes]], 0)
        scores = lax.dot_general(query, keys, (((1,), (1,)), ((), ())), preferred_element_type=F32) * (
            1.0 / math.sqrt(HD)
        )
        parts = []
        for i in range(SPAN):
            seen = scores[:, i * count : (i + 1) * count]
            parts.append(jnp.where(block >= SPAN - i, seen, -1e30))
        parts.append(jnp.where(causal, scores[:, SPAN * count :], -1e30))
        scores = jnp.concatenate(parts, 1)
        top = jnp.max(scores, axis=1, keepdims=True)
        probs = jnp.exp(scores - top)
        total = jnp.sum(probs, axis=1, keepdims=True)
        numer = mm(probs.astype(BF16), values)
        branch = numer / total
        out_ref[:, lanes] = branch
        squares = squares + branch * branch
    sum_ref[...] = squares.T


def attend(block, query, key, value, one, two, three):
    count, width = query.shape
    vmem = pl.BlockSpec(memory_space=pltpu.VMEM)
    return pl.pallas_call(
        attention_body,
        out_shape=(jax.ShapeDtypeStruct((count, width), F32), jax.ShapeDtypeStruct((HD, count), F32)),
        in_specs=[pl.BlockSpec(memory_space=pltpu.SMEM)] + [vmem] * 6,
        out_specs=(vmem, vmem),
        compiler_params=pltpu.CompilerParams(vmem_limit_bytes=VMEM_LIMIT),
        name="attention",
    )(block, query, key, value, one, two, three)


def sums_body(returned_ref, query_t_ref, att_ref, out_ref):
    mixed = returned_ref[...].astype(F32).reshape(query_t_ref.shape) * query_t_ref[...].astype(F32)
    mixer = jnp.sum(mixed * mixed, axis=0, keepdims=True)
    attention = jnp.sum(att_ref[...], axis=0, keepdims=True)
    rows = jnp.concatenate(
        [attention[:, :RADIX], attention[:, RADIX:], mixer[:, :RADIX], mixer[:, RADIX:], jnp.zeros((4, RADIX), F32)], 0
    )
    out_ref[...] = jnp.broadcast_to(rows[None], out_ref.shape)


def mixed_body(returned_ref, query_ref, beta_ref, out_ref):
    count, width = query_ref.shape
    returned = returned_ref[...].astype(F32).reshape(width, count).T
    out_ref[...] = query_ref[...].astype(F32) * returned * beta_ref[...]


def join_body(sums_ref, att_ref, mixed_ref, beta_ref, out_ref):
    count, _ = att_ref.shape
    total = sums_ref[0]
    for peer in range(1, sums_ref.shape[0]):
        total = total + sums_ref[peer]
    scale = lax.rsqrt(total * (1.0 / D) + 1e-05) * 0.5
    columns = jnp.concatenate([scale, jnp.zeros((RADIX - 8, RADIX), F32)], 0).T
    for h in range(count // RADIX):
        rows = slice(h * RADIX, (h + 1) * RADIX)
        attention_scale = columns[:, h : h + 1]
        mixer_scale = columns[:, 2 + h : 3 + h]
        out_ref[rows, :] = (
            beta_ref[...] * att_ref[rows, :] * attention_scale + mixed_ref[rows, :] * mixer_scale
        ).astype(BF16)


def transpose_body(in_ref, out_ref):
    out_ref[...] = in_ref[...].astype(F32).T.astype(BF16)


def mixer(
    mixer_query,
    mixer_key,
    mixer_value,
    shift_taps,
    conv_kernel,
    heads_query,
    heads_key,
    heads_value,
    beta_attention,
    beta_mixer,
):
    count, width = mixer_key.shape
    blocks = lax.axis_size("seq")
    peers = lax.axis_size("head")
    channels = width // blocks
    sds = jax.ShapeDtypeStruct
    tables = conv_tables(count)
    onward = [(i, i + 1) for i in range(blocks - 1)]
    seq = lax.axis_index("seq")

    signal = kernel_call(
        shift_body, sds((blocks, channels // SIDE, SIDE * count + RADIX), BF16), [pltpu.VMEM((count + 8, width), F32)]
    )(mixer_key, mixer_value, shift_taps)
    received = lax.all_to_all(signal, "seq", 0, 0, tiled=True)
    own_taps = lax.dynamic_slice(shift_taps, (0, seq * channels), (TAPS, channels)).T
    rows = pltpu.VMEM((channels * RADIX, RADIX), F32)
    kernel_spectrum = pl.pallas_call(
        functools.partial(kernel_spectrum_body, count // RADIX),
        out_shape=sds((channels * RADIX, 2 * RADIX), F32),
        in_specs=[pl.BlockSpec(memory_space=pltpu.HBM), pl.BlockSpec(memory_space=pltpu.VMEM)],
        scratch_shapes=[rows, pltpu.VMEM(conv_kernel.shape, F32), pltpu.SemaphoreType.DMA],
        compiler_params=pltpu.CompilerParams(vmem_limit_bytes=VMEM_LIMIT),
        name="kernel_spectrum",
    )(pltpu.with_memory_space_constraint(conv_kernel, pltpu.HBM), tables)
    filtered = kernel_call(
        filter_body, sds((blocks, channels, count), BF16), [rows, rows]
    )(received, own_taps, kernel_spectrum, tables)
    returned = lax.all_to_all(filtered, "seq", 0, 0, tiled=True)

    own = pack(heads_key, heads_value)
    two_back = lax.ppermute(own, "seq", [(i, i + 2) for i in range(blocks - 2)])
    three_back = lax.ppermute(two_back, "seq", onward)
    two_back, three_back = lax.optimization_barrier((two_back, three_back))
    odd = seq % 2 == 1
    exchanged = jnp.concatenate(
        [jnp.where(odd, two_back[:count], heads_key), jnp.where(odd, two_back[count:], heads_value)], 0
    )
    one_back = lax.ppermute(exchanged, "seq", [(i, i ^ 1) for i in range(blocks)])
    block = seq.astype(jnp.int32).reshape(1)
    attention_branch, attention_squares = attend(block, heads_query, heads_key, heads_value, one_back, two_back, three_back)
    query_t = kernel_call(transpose_body, sds((width, count), BF16))(mixer_query)
    sums = kernel_call(sums_body, sds((peers, 8, RADIX), F32))(returned, query_t, attention_squares)
    gathered = lax.all_to_all(sums, "head", 0, 0, tiled=True)
    mixed = kernel_call(mixed_body, sds((count, width), F32))(
        returned, mixer_query, beta_mixer[None, :]
    )
    return kernel_call(join_body, sds((count, width), BF16))(gathered, attention_branch, mixed, beta_attention[None, :])


def solution(mesh):
    return jax.shard_map(
        mixer,
        mesh=mesh,
        in_specs=(
            P("seq", "head"),
            P("seq", "head"),
            P("seq", "head"),
            P(None, "head"),
            P(("head", "seq"), None),
            P("seq", "head"),
            P("seq", "head"),
            P("seq", "head"),
            P("head"),
            P("head"),
        ),
        out_specs=P("seq", "head"),
        check_vma=False,
    )
```

```python
import functools
import math

import jax
import jax.numpy as jnp
import numpy as np
from jax import lax
from jax.experimental import pallas as pl
from jax.experimental.pallas import tpu as pltpu
from jax.sharding import PartitionSpec as P


D = 4096
HD = 128
TAPS = 8
SPAN = 3
SIDE = 4
RADIX = 128
VMEM_LIMIT = 20 * 2**20
F32 = jnp.float32
BF16 = jnp.bfloat16


def split_table(table):
    high = table.astype(np.float32).astype(jnp.bfloat16)
    low = (table - high.astype(np.float64)).astype(np.float32).astype(jnp.bfloat16)
    return high, low


def conv_tables(tokens):
    half = tokens // RADIX
    place = np.arange(RADIX)
    order = (place % (RADIX // half)) * half + place // (RADIX // half)
    freq = np.arange(RADIX) + 0.5
    one = 2.0 * np.pi * np.outer(freq, order) / (2 * RADIX)
    first = np.concatenate([np.cos(one), -np.sin(one)], 0)
    last = first.T * (1.0 / (RADIX * RADIX))
    twist = 2.0 * np.pi * np.outer(freq, place) / (2 * RADIX * RADIX)
    two = 2.0 * np.pi * np.outer(place, place) / RADIX
    cos, sin = np.cos(two), np.sin(two)
    ahead = np.block([[cos, -sin], [sin, cos]])
    back = np.block([[cos, sin], [-sin, cos]])
    products = [
        np.concatenate(split_table(first), 1),
        np.concatenate(split_table(last), 0),
        *split_table(ahead),
        *split_table(back),
        np.concatenate(split_table(np.concatenate([np.cos(twist), np.sin(twist)], 1)), 0),
    ]
    return jnp.asarray(np.stack(products))


def halves(value):
    high = value.astype(BF16)
    return high, (value - high.astype(F32)).astype(BF16)


def mm(left, right):
    return lax.dot_general(left, right, (((1,), (0,)), ((), ())), preferred_element_type=F32)


def kernel_call(body, out_shape, scratch=()):
    def call(*args):
        return pl.pallas_call(
            body,
            out_shape=out_shape,
            scratch_shapes=list(scratch),
            compiler_params=pltpu.CompilerParams(vmem_limit_bytes=VMEM_LIMIT),
        )(*args)

    return call


def shift_body(key_ref, value_ref, taps_ref, out_ref, ext_ref):
    count, width = key_ref.shape
    ext_ref[0:8, :] = jnp.zeros((8, width), F32)
    ext_ref[8 : 8 + count, :] = key_ref[...].astype(F32)
    taps = taps_ref[...]
    total = taps[0:1, :] * ext_ref[8 : 8 + count, :]
    for j in range(1, TAPS):
        total = total + taps[j : j + 1, :] * ext_ref[8 - j : 8 - j + count, :]
    product = total * value_ref[...].astype(F32)
    edges = jnp.concatenate(
        [
            ext_ref[8:16, :],
            ext_ref[count : 8 + count, :],
            value_ref[0:16, :].astype(F32)[0:8],
            jnp.zeros((RADIX - 24, width), F32),
        ],
        0,
    )
    blocks, lines = out_ref.shape[:2]
    product = product.T.reshape(blocks, SIDE, lines, count)
    edges = edges.T.reshape(blocks, SIDE, lines, RADIX)
    for i in range(SIDE):
        out_ref[:, :, i * count : (i + 1) * count] = product[:, i].astype(BF16)
    joined = jnp.concatenate([edges[:, i, :, : RADIX // SIDE] for i in range(SIDE)], 2)
    out_ref[:, :, SIDE * count :] = joined.astype(BF16)


def pack_body(key_in, value_in, out_ref, sems):
    count = key_in.shape[0]
    copies = [
        pltpu.make_async_copy(source, out_ref.at[pl.ds(i * count, count)], sems.at[i])
        for i, source in enumerate((key_in, value_in))
    ]
    for copy in copies:
        copy.start()
    for copy in copies:
        copy.wait()


def pack(key, value):
    count, width = key.shape
    return pl.pallas_call(
        pack_body,
        out_shape=jax.ShapeDtypeStruct((2 * count, width), key.dtype),
        in_specs=[pl.BlockSpec(memory_space=pltpu.HBM)] * 2,
        out_specs=pl.BlockSpec(memory_space=pltpu.VMEM),
        scratch_shapes=[pltpu.SemaphoreType.DMA((2,))],
        compiler_params=pltpu.CompilerParams(vmem_limit_bytes=VMEM_LIMIT),
        name="pack",
    )(*(pltpu.with_memory_space_constraint(x, pltpu.HBM) for x in (key, value)))


def product3(value, table_hi, table_lo):
    high, low = halves(value)
    return mm(high, table_hi) + mm(low, table_hi) + mm(high, table_lo)


def twists(tables_ref):
    table = tables_ref[6].astype(F32)
    table = table[:RADIX] + table[RADIX:]
    return table[:, :RADIX], table[:, RADIX:]


def spectrum(step, tables_ref):
    cos, sin = twists(tables_ref)
    turned = []
    for c in range(step.shape[1] // RADIX):
        lanes = slice(c * RADIX, (c + 1) * RADIX)
        real, imag = step[:RADIX, lanes], step[RADIX:, lanes]
        turned.append(jnp.concatenate([real * cos + imag * sin, imag * cos - real * sin], 1))
    return product3(jnp.concatenate(turned, 0), tables_ref[2], tables_ref[3])


def gather_rows(rows_ref, channels):
    return jnp.concatenate([rows_ref[pl.ds(c, RADIX, stride=channels), :] for c in range(channels)], 1)


def kernel_spectrum_body(half, kernel_in, tables_ref, out_ref, rows_ref, kernel_ref, sem):
    channels = kernel_ref.shape[0]
    copy = pltpu.make_async_copy(kernel_in, kernel_ref, sem)
    copy.start()
    copy.wait()
    for a in range(RADIX):
        row = ((a % half) * (RADIX // half) + a // half) * channels
        rows_ref[row : row + channels, :] = kernel_ref[:, a * RADIX : (a + 1) * RADIX]
    high, low = halves(gather_rows(rows_ref, channels))
    step = mm(tables_ref[0], jnp.concatenate([high, high], 0)) + mm(tables_ref[0, :, :RADIX], low)
    out_ref[...] = spectrum(step, tables_ref)


def channel_rows(signal_ref, count, h):
    return jnp.concatenate(
        [signal_ref[:, :, i * count + h * RADIX : i * count + (h + 1) * RADIX].astype(F32) for i in range(SIDE)], 1
    )


def first_tokens(signal_ref, taps_ref, count):
    own = signal_ref[:, :, SIDE * count :].astype(F32)
    own = jnp.concatenate([own] + [jnp.roll(own, -i * (RADIX // SIDE), 2) for i in range(1, SIDE)], 1)
    head = channel_rows(signal_ref, count, 0)
    previous = jnp.concatenate([jnp.zeros_like(own[:1]), own[:-1]], 0)
    sources, channels = own.shape[:2]
    own, previous, head = (x.reshape(sources * channels, RADIX) for x in (own, previous, head))
    lane = lax.broadcasted_iota(jnp.int32, own.shape, 1)
    window = jnp.where(lane < 16, previous, pltpu.roll(own, 16, 1))
    total = jnp.zeros_like(window)
    for j in range(TAPS):
        tap = jnp.broadcast_to(taps_ref[:, j : j + 1], (channels, RADIX))[None]
        tap = jnp.broadcast_to(tap, (sources, channels, RADIX)).reshape(window.shape)
        total = total + tap * (pltpu.roll(window, j, 1) if j else window)
    return jnp.where(lane < 8, pltpu.roll(total * own, RADIX - 16, 1), head)


def filter_body(signal_ref, taps_ref, spec_ref, tables_ref, out_ref, rows_ref, back_ref):
    sources, channels, count = out_ref.shape
    half = count // RADIX
    rows = sources * channels
    rows_ref[:rows, :] = first_tokens(signal_ref, taps_ref, count)
    for h in range(1, half):
        part = channel_rows(signal_ref, count, h)
        rows_ref[h * rows : (h + 1) * rows, :] = part.reshape(rows, RADIX)
    data = gather_rows(rows_ref, channels).astype(BF16)
    step = mm(tables_ref[0], jnp.concatenate([data, data], 0))
    both = spectrum(step, tables_ref)
    sig_r, sig_i = both[:, :RADIX], both[:, RADIX:]
    ker_r, ker_i = spec_ref[:, :RADIX], spec_ref[:, RADIX:]
    both = jnp.concatenate([sig_r * ker_r - sig_i * ker_i, sig_r * ker_i + sig_i * ker_r], 1)
    both = product3(both, tables_ref[4], tables_ref[5])
    cos, sin = twists(tables_ref)
    turned = []
    for c in range(channels):
        lines = slice(c * RADIX, (c + 1) * RADIX)
        real, imag = both[lines, :RADIX], both[lines, RADIX:]
        turned.append(jnp.concatenate([real * cos - imag * sin, imag * cos + real * sin], 0))
    high, low = halves(jnp.concatenate(turned, 1))
    both = mm(tables_ref[1], high)
    result = both[:RADIX] + both[RADIX:] + mm(tables_ref[1, :RADIX], low)
    for c in range(channels):
        back_ref[pl.ds(c, RADIX, stride=channels), :] = result[:, c * RADIX : (c + 1) * RADIX]
    for h in range(half):
        part = back_ref[h * rows : (h + 1) * rows, :].astype(BF16)
        out_ref[:, :, h * RADIX : (h + 1) * RADIX] = part.reshape(sources, channels, RADIX)


def attention_body(block_ref, query_ref, key_ref, value_ref, one_ref, two_ref, three_ref, out_ref, sum_ref):
    count, width = query_ref.shape
    block = block_ref[0]
    earlier = (three_ref, two_ref, one_ref)
    row = lax.broadcasted_iota(jnp.int32, (count, count), 0)
    col = lax.broadcasted_iota(jnp.int32, (count, count), 1)
    causal = col <= row
    squares = jnp.zeros((count, HD), F32)
    for h in range(width // HD):
        lanes = slice(h * HD, (h + 1) * HD)
        query = query_ref[:, lanes]
        keys = jnp.concatenate([ref[0:count, lanes] for ref in earlier] + [key_ref[:, lanes]], 0)
        values = jnp.concatenate([ref[count:, lanes] for ref in earlier] + [value_ref[:, lanes]], 0)
        scores = lax.dot_general(query, keys, (((1,), (1,)), ((), ())), preferred_element_type=F32) * (
            1.0 / math.sqrt(HD)
        )
        parts = []
        for i in range(SPAN):
            seen = scores[:, i * count : (i + 1) * count]
            parts.append(jnp.where(block >= SPAN - i, seen, -1e30))
        parts.append(jnp.where(causal, scores[:, SPAN * count :], -1e30))
        scores = jnp.concatenate(parts, 1)
        top = jnp.max(scores, axis=1, keepdims=True)
        probs = jnp.exp(scores - top)
        total = jnp.sum(probs, axis=1, keepdims=True)
        numer = mm(probs.astype(BF16), values)
        branch = numer / total
        out_ref[:, lanes] = branch
        squares = squares + branch * branch
    sum_ref[...] = squares.T


def attend(block, query, key, value, one, two, three):
    count, width = query.shape
    vmem = pl.BlockSpec(memory_space=pltpu.VMEM)
    return pl.pallas_call(
        attention_body,
        out_shape=(jax.ShapeDtypeStruct((count, width), F32), jax.ShapeDtypeStruct((HD, count), F32)),
        in_specs=[pl.BlockSpec(memory_space=pltpu.SMEM)] + [vmem] * 6,
        out_specs=(vmem, vmem),
        compiler_params=pltpu.CompilerParams(vmem_limit_bytes=VMEM_LIMIT),
        name="attention",
    )(block, query, key, value, one, two, three)


def sums_body(returned_ref, query_t_ref, att_ref, out_ref):
    mixed = returned_ref[...].astype(F32).reshape(query_t_ref.shape) * query_t_ref[...].astype(F32)
    mixer = jnp.sum(mixed * mixed, axis=0, keepdims=True)
    attention = jnp.sum(att_ref[...], axis=0, keepdims=True)
    rows = jnp.concatenate(
        [attention[:, :RADIX], attention[:, RADIX:], mixer[:, :RADIX], mixer[:, RADIX:]], 0
    )
    out_ref[...] = jnp.broadcast_to(rows[None], out_ref.shape)


def mixed_body(returned_ref, query_ref, beta_ref, out_ref):
    count, width = query_ref.shape
    returned = returned_ref[...].astype(F32).reshape(width, count).T
    out_ref[...] = query_ref[...].astype(F32) * returned * beta_ref[...]


def join_body(sums_ref, att_ref, mixed_ref, beta_ref, out_ref):
    count, _ = att_ref.shape
    total = sums_ref[0]
    for peer in range(1, sums_ref.shape[0]):
        total = total + sums_ref[peer]
    scale = lax.rsqrt(total * (1.0 / D) + 1e-05) * 0.5
    columns = jnp.concatenate([scale, jnp.zeros((RADIX - 4, RADIX), F32)], 0).T
    for h in range(count // RADIX):
        rows = slice(h * RADIX, (h + 1) * RADIX)
        attention_scale = columns[:, h : h + 1]
        mixer_scale = columns[:, 2 + h : 3 + h]
        out_ref[rows, :] = (
            beta_ref[...] * att_ref[rows, :] * attention_scale + mixed_ref[rows, :] * mixer_scale
        ).astype(BF16)


def transpose_body(in_ref, out_ref):
    out_ref[...] = in_ref[...].astype(F32).T.astype(BF16)


def mixer(
    mixer_query,
    mixer_key,
    mixer_value,
    shift_taps,
    conv_kernel,
    heads_query,
    heads_key,
    heads_value,
    beta_attention,
    beta_mixer,
):
    count, width = mixer_key.shape
    blocks = lax.axis_size("seq")
    peers = lax.axis_size("head")
    channels = width // blocks
    sds = jax.ShapeDtypeStruct
    tables = conv_tables(count)
    onward = [(i, i + 1) for i in range(blocks - 1)]
    seq = lax.axis_index("seq")

    signal = kernel_call(
        shift_body, sds((blocks, channels // SIDE, SIDE * count + RADIX), BF16), [pltpu.VMEM((count + 8, width), F32)]
    )(mixer_key, mixer_value, shift_taps)
    received = lax.all_to_all(signal, "seq", 0, 0, tiled=True)
    own_taps = lax.dynamic_slice(shift_taps, (0, seq * channels), (TAPS, channels)).T
    rows = pltpu.VMEM((channels * RADIX, RADIX), F32)
    kernel_spectrum = pl.pallas_call(
        functools.partial(kernel_spectrum_body, count // RADIX),
        out_shape=sds((channels * RADIX, 2 * RADIX), F32),
        in_specs=[pl.BlockSpec(memory_space=pltpu.HBM), pl.BlockSpec(memory_space=pltpu.VMEM)],
        scratch_shapes=[rows, pltpu.VMEM(conv_kernel.shape, F32), pltpu.SemaphoreType.DMA],
        compiler_params=pltpu.CompilerParams(vmem_limit_bytes=VMEM_LIMIT),
        name="kernel_spectrum",
    )(pltpu.with_memory_space_constraint(conv_kernel, pltpu.HBM), tables)
    filtered = kernel_call(
        filter_body, sds((blocks, channels, count), BF16), [rows, rows]
    )(received, own_taps, kernel_spectrum, tables)
    returned = lax.all_to_all(filtered, "seq", 0, 0, tiled=True)

    own = pack(heads_key, heads_value)
    two_back = lax.ppermute(own, "seq", [(i, i + 2) for i in range(blocks - 2)])
    three_back = lax.ppermute(two_back, "seq", onward)
    two_back, three_back = lax.optimization_barrier((two_back, three_back))
    odd = seq % 2 == 1
    exchanged = jnp.concatenate(
        [jnp.where(odd, two_back[:count], heads_key), jnp.where(odd, two_back[count:], heads_value)], 0
    )
    one_back = lax.ppermute(exchanged, "seq", [(i, i ^ 1) for i in range(blocks)])
    block = seq.astype(jnp.int32).reshape(1)
    attention_branch, attention_squares = attend(block, heads_query, heads_key, heads_value, one_back, two_back, three_back)
    query_t = kernel_call(transpose_body, sds((width, count), BF16))(mixer_query)
    sums = kernel_call(sums_body, sds((peers, 4, RADIX), F32))(returned, query_t, attention_squares)
    gathered = lax.all_to_all(sums, "head", 0, 0, tiled=True)
    mixed = kernel_call(mixed_body, sds((count, width), F32))(
        returned, mixer_query, beta_mixer[None, :]
    )
    return kernel_call(join_body, sds((count, width), BF16))(gathered, attention_branch, mixed, beta_attention[None, :])


def solution(mesh):
    return jax.shard_map(
        mixer,
        mesh=mesh,
        in_specs=(
            P("seq", "head"),
            P("seq", "head"),
            P("seq", "head"),
            P(None, "head"),
            P(("head", "seq"), None),
            P("seq", "head"),
            P("seq", "head"),
            P("seq", "head"),
            P("head"),
            P("head"),
        ),
        out_specs=P("seq", "head"),
        check_vma=False,
    )
```
